256 devices in a mesh: gx: 8 (over x, core), gy: 32 (over y, z).
Axes of the slice: x: 4, y: 4, z: 8, core: 2. Of those that a mesh axis runs over, the one named last changes fastest.
Arguments:
- features: float32 [64, 524288], P(None, ('gx', 'gy')), may hold values from -6 to 6
- cotangent: float32 [64, 524288], P(None, ('gx', 'gy')), may hold values from -6 to 6
- edge_src: int32 [8, 524288], P(None, ('gx', 'gy')), may hold values from 0 to 2559
- send_rows: int32 [4, 32768], P(None, ('gx', 'gy')), may hold values from 0 to 2047
- fine_to_coarse: int32 [524288], P(('gx', 'gy')), may hold values from 0 to 2047
- coarse_to_fine: int32 [524288], P(('gx', 'gy')), may hold values from 0 to 2047
- coarse_edges: int32 [2, 8192], replicated, may hold values from 0 to 2047
- edge_in: float32 [64, 128], replicated, may hold values from -0.5 to 0.5
- edge_out: float32 [64, 64], replicated, may hold values from -0.75 to 0.75
- node_in: float32 [64, 128], replicated, may hold values from -0.5 to 0.5
- node_out: float32 [64, 64], replicated, may hold values from -0.75 to 0.75
- coarse_in: float32 [64, 64], replicated, may hold values from -0.75 to 0.75
- coarse_out: float32 [64, 64], replicated, may hold values from -0.75 to 0.75
- coarse_mix: float32 [64, 64], replicated, may hold values from -0.75 to 0.75
- up_in: float32 [64, 128], replicated, may hold values from -0.5 to 0.5
- up_out: float32 [64, 64], replicated, may hold values from -0.75 to 0.75
- biases: float32 [4, 64], replicated, may hold values from -3 to 3
Outputs:
- output: float32 [64, 524288], P(None, ('gx', 'gy'))
- grad_features: float32 [64, 524288], P(None, ('gx', 'gy'))
- grad_edge_in: float32 [64, 128], replicated
- grad_edge_out: float32 [64, 64], replicated
- grad_node_in: float32 [64, 128], replicated
- grad_node_out: float32 [64, 64], replicated
- grad_coarse_in: float32 [64, 64], replicated
- grad_coarse_out: float32 [64, 64], replicated
- grad_coarse_mix: float32 [64, 64], replicated
- grad_up_in: float32 [64, 128], replicated
- grad_up_out: float32 [64, 64], replicated
- grad_biases: float32 [4, 64], replicated
The draws below stay inside these ranges and needn't reach their ends.
Inputs may be any that keep to these rules, and one draw needn't show every extreme that they name: `edge_src`: indexes the receiver partition's 2048 own nodes, then the four received packets in the order of the first step. `send_rows`: partition-local node numbers.
All inputs are finite; a program needn't handle non-finite values.
Results may differ from the reference program's by a relative error of at most 0.0003.
Values sent between devices are 32-bit elements; how exact they have to be, the bound alone decides.
A program may use at most 64 MiB of HBM per device.

```python
from functools import partial
import jax
import jax.numpy as jnp
from jax import lax

LAT = 64
HID = 64
DEG = 8
NODE_DEV = 2048
COARSE = 2048
CEDGES = 8192
HALO = 128
NODES = 524288
HALOS = 32768
N_GX = 8
N_GY = 32


def touch_ends(drawn, key, low, top_value):
    extent = drawn.shape
    spot = [jax.random.randint(jax.random.fold_in(key, axis), (), 0, extent[axis]) for axis in range(len(extent))]
    drawn = drawn.at[tuple(spot)].set(low)
    longest = extent.index(max(extent))
    spot[longest] = (spot[longest] + 1) % extent[longest]
    return drawn.at[tuple(spot)].set(top_value)


def block_scale(rng, extent, cuts, smallest, largest):
    gain = 1.0
    for position, blocks in cuts:
        steps = jax.random.uniform(jax.random.fold_in(jax.random.fold_in(rng, 6), position), (blocks,), jnp.float32, smallest / len(cuts), largest / len(cuts))
        gain = gain * jnp.repeat(jnp.exp(steps), extent[position] // blocks).reshape((-1,) + (1,) * (len(extent) - 1 - position))
    return gain


def centred(own_key, extent, width, limit, split=(), dtype=jnp.bfloat16):
    drawn = width * jax.random.normal(own_key, extent, jnp.float32)
    if split:
        drawn = drawn * block_scale(own_key, extent, split, -0.22, 0.18)
    return jnp.clip(drawn, -limit, limit).astype(dtype)


def setup_inputs(seed: int = 0) -> dict:
    key_of = jax.random.split(jax.random.key(seed), 18)
    features = centred(key_of[0], (LAT, NODES), 1.0, 6.0, ((1, 256),), jnp.float32)
    cotangent = centred(key_of[1], (LAT, NODES), 1.0, 6.0, ((1, 256),), jnp.float32)
    edge_src = touch_ends(jax.random.randint(key_of[2], (DEG, NODES), 0, NODE_DEV + 4 * HALO), jax.random.fold_in(key_of[2], 1), 0, (NODE_DEV + 4 * HALO) - 1).astype(jnp.int32)
    send_rows = touch_ends(jax.random.randint(key_of[3], (4, HALOS), 0, NODE_DEV), jax.random.fold_in(key_of[3], 1), 0, NODE_DEV - 1).astype(jnp.int32)
    fine_to_coarse = touch_ends(jax.random.randint(key_of[4], (NODES,), 0, COARSE), jax.random.fold_in(key_of[4], 1), 0, COARSE - 1).astype(jnp.int32)
    coarse_to_fine = touch_ends(jax.random.randint(key_of[5], (NODES,), 0, COARSE), jax.random.fold_in(key_of[5], 1), 0, COARSE - 1).astype(jnp.int32)
    coarse_edges = touch_ends(jax.random.randint(key_of[6], (2, CEDGES), 0, COARSE), jax.random.fold_in(key_of[6], 1), 0, COARSE - 1).astype(jnp.int32)
    edge_in = centred(key_of[7], (HID, 2 * LAT), (2 * LAT) ** -0.5, 0.5, (), jnp.float32)
    edge_out = centred(key_of[8], (LAT, HID), HID ** -0.5, 0.75, (), jnp.float32)
    node_in = centred(key_of[9], (HID, 2 * LAT), (2 * LAT) ** -0.5, 0.5, (), jnp.float32)
    node_out = centred(key_of[10], (LAT, HID), HID ** -0.5, 0.75, (), jnp.float32)
    coarse_in = centred(key_of[11], (HID, LAT), LAT ** -0.5, 0.75, (), jnp.float32)
    coarse_out = centred(key_of[12], (LAT, HID), HID ** -0.5, 0.75, (), jnp.float32)
    coarse_mix = centred(key_of[13], (LAT, LAT), LAT ** -0.5, 0.75, (), jnp.float32)
    up_in = centred(key_of[14], (HID, 2 * LAT), (2 * LAT) ** -0.5, 0.5, (), jnp.float32)
    up_out = centred(key_of[15], (LAT, HID), HID ** -0.5, 0.75, (), jnp.float32)
    biases = centred(key_of[16], (4, HID), 0.5, 3.0, (), jnp.float32)
    return {"features": features, "cotangent": cotangent, "edge_src": edge_src, "send_rows": send_rows, "fine_to_coarse": fine_to_coarse, "coarse_to_fine": coarse_to_fine, "coarse_edges": coarse_edges, "edge_in": edge_in, "edge_out": edge_out, "node_in": node_in, "node_out": node_out, "coarse_in": coarse_in, "coarse_out": coarse_out, "coarse_mix": coarse_mix, "up_in": up_in, "up_out": up_out, "biases": biases}


def matmul(left_side, right_side):
    return jnp.dot(left_side, right_side, precision=lax.Precision.HIGHEST, preferred_element_type=jnp.float32)

def swish(values):
    return values * jax.nn.sigmoid(values)

def fine_update(latent, extended, edge_in, edge_out, node_in, node_out, edge_bias, node_bias, sources):
    feature_count = latent.shape[0]
    receiver_part = matmul(edge_in[:, :feature_count], latent)
    sender_part = matmul(edge_in[:, feature_count:], extended)
    hidden = swish(receiver_part[:, None, :] + sender_part[:, sources] + edge_bias[:, None, None])
    summed = matmul(edge_out, lax.optimization_barrier(jnp.sum(hidden, axis=1)))
    activation = swish(matmul(node_in[:, :feature_count], latent) + matmul(node_in[:, feature_count:], summed) + node_bias[:, None])
    return latent + matmul(node_out, activation)

def coarse_node(pooled, coarse_in, coarse_out, coarse_bias):
    return pooled + matmul(coarse_out, swish(matmul(coarse_in, pooled) + coarse_bias[:, None]))

def coarse_edge(nodes, coarse_mix, coarse_edges):
    gathered = nodes[:, coarse_edges[0]]
    summed = jnp.zeros_like(nodes).at[:, coarse_edges[1]].add(gathered)
    factor = (nodes.shape[1] / coarse_edges.shape[1]) ** 0.5
    return nodes + matmul(coarse_mix, summed) * factor

def up_update(middle, looked, up_in, up_out, up_bias):
    feature_count = middle.shape[0]
    activation = swish(matmul(up_in[:, :feature_count], middle) + matmul(up_in[:, feature_count:], looked) + up_bias[:, None])
    return middle + matmul(up_out, activation)

def forward(features, edge_in, edge_out, node_in, node_out, coarse_in, coarse_out, coarse_mix, up_in, up_out, biases, edge_src, send_rows, fine_to_coarse, coarse_to_fine, coarse_edges):
    count = N_GX * N_GY
    grid = features.reshape(LAT, N_GX, N_GY, NODE_DEV)
    rows = send_rows.reshape(4, N_GX, N_GY, HALO)
    packets = []
    for direction in range(4):
        index = jnp.broadcast_to(rows[direction][None], (LAT, N_GX, N_GY, HALO))
        packets.append(jnp.take_along_axis(grid, index, axis=3))
    below_x = jnp.pad(packets[0], ((0, 0), (1, 0), (0, 0), (0, 0)))[:, :-1]
    above_x = jnp.pad(packets[1], ((0, 0), (0, 1), (0, 0), (0, 0)))[:, 1:]
    below_y = jnp.pad(packets[2], ((0, 0), (0, 0), (1, 0), (0, 0)))[:, :, :-1]
    above_y = jnp.pad(packets[3], ((0, 0), (0, 0), (0, 1), (0, 0)))[:, :, 1:]
    extended = jnp.concatenate([grid, below_x, above_x, below_y, above_y], axis=3)
    width_ext = NODE_DEV + 4 * HALO
    latent_dev = grid.reshape(LAT, count, NODE_DEV).transpose(1, 0, 2)
    extended_dev = extended.reshape(LAT, count, width_ext).transpose(1, 0, 2)
    sources_dev = edge_src.reshape(DEG, count, NODE_DEV).transpose(1, 0, 2)
    update = jax.checkpoint(fine_update)

    def one_partition(items):
        return update(items[0], items[1], edge_in, edge_out, node_in, node_out, biases[0], biases[1], items[2])
    middle_dev = lax.map(one_partition, (latent_dev, extended_dev, sources_dev))
    middle = middle_dev.transpose(1, 0, 2).reshape(LAT, NODE_DEV * count)
    pool_scale = (COARSE / (NODE_DEV * count)) ** 0.5
    pooled = jnp.zeros((LAT, COARSE), jnp.float32).at[:, fine_to_coarse].add(middle) * pool_scale
    nodes = coarse_node(pooled, coarse_in, coarse_out, biases[2])
    mixed = coarse_edge(nodes, coarse_mix, coarse_edges)
    looked = mixed[:, coarse_to_fine]
    return up_update(middle, looked, up_in, up_out, biases[3])

def reference(features, cotangent, edge_src, send_rows, fine_to_coarse, coarse_to_fine, coarse_edges, edge_in, edge_out, node_in, node_out, coarse_in, coarse_out, coarse_mix, up_in, up_out, biases):
    closed = partial(forward, edge_src=edge_src, send_rows=send_rows, fine_to_coarse=fine_to_coarse, coarse_to_fine=coarse_to_fine, coarse_edges=coarse_edges)
    output, backward = jax.vjp(closed, features, edge_in, edge_out, node_in, node_out, coarse_in, coarse_out, coarse_mix, up_in, up_out, biases)
    grads = backward(cotangent)
    return (output, grads[0], grads[1], grads[2], grads[3], grads[4], grads[5], grads[6], grads[7], grads[8], grads[9], grads[10])
```

```python
from functools import partial
import math

import jax
import jax.numpy as jnp
from jax import lax
from jax.experimental import pallas as pl
from jax.experimental.pallas import tpu as pltpu
from jax.sharding import PartitionSpec as P

COARSE = 2048
MESH = pl.DeviceIdType.MESH


def add_up_kernel(tiles, x_ref, o_ref, parts, row_sum, tile_parts, tile_sum, full,
                  send1, recv1, send2, recv2, send3, recv3, send4, recv4):
    gx, gy = lax.axis_index("gx"), lax.axis_index("gy")
    barrier = pltpu.get_barrier_semaphore()

    def greet_row(k, carry):
        pl.semaphore_signal(barrier, inc=1, device_id=(lax.rem(gx + k, 8), gy), device_id_type=MESH)
        return carry

    def greet_col(k, carry):
        pl.semaphore_signal(barrier, inc=1, device_id=(gx, lax.rem(gy + k, 32)), device_id_type=MESH)
        return carry

    lax.fori_loop(1, 8, greet_row, 0)
    lax.fori_loop(1, 32, greet_col, 0)
    pl.semaphore_wait(barrier, 38)

    def scatter_row(k):
        peer = lax.rem(gx + k, 8)
        return pltpu.make_async_remote_copy(
            src_ref=x_ref.at[pl.ds(pl.multiple_of(peer * 8, 8), 8)], dst_ref=parts.at[k],
            send_sem=send1.at[k], recv_sem=recv1.at[k],
            device_id=(peer, gy), device_id_type=MESH)

    def scatter_col(k):
        peer = lax.rem(gy + k, 32)
        return pltpu.make_async_remote_copy(
            src_ref=row_sum.at[lax.rem(peer, tiles)], dst_ref=tile_parts.at[gy],
            send_sem=send2.at[k], recv_sem=recv2.at[k],
            device_id=(gx, peer), device_id_type=MESH)

    mine = lax.rem(gy, tiles)
    block = gy - mine

    def gather_col(k):
        peer = block + lax.rem(mine + k, tiles)
        return pltpu.make_async_remote_copy(
            src_ref=tile_sum.at[mine], dst_ref=tile_sum.at[mine],
            send_sem=send3.at[k], recv_sem=recv3.at[k],
            device_id=(gx, peer), device_id_type=MESH)

    rows = pl.ds(pl.multiple_of(gx * 8, 8), 8)

    def gather_row(k):
        return pltpu.make_async_remote_copy(
            src_ref=full.at[rows], dst_ref=full.at[rows],
            send_sem=send4.at[k], recv_sem=recv4.at[k],
            device_id=(lax.rem(gx + k, 8), gy), device_id_type=MESH)

    def start_all(make, count):
        def body(k, carry):
            make(k).start()
            return carry
        lax.fori_loop(1, count, body, 0)

    def wait_all(make, count):
        def body(k, carry):
            make(k).wait()
            return carry
        lax.fori_loop(1, count, body, 0)

    start_all(scatter_row, 8)
    wait_all(scatter_row, 8)
    total = x_ref[rows]
    for k in range(1, 8):
        total = total + parts[k]
    for tile in range(tiles):
        row_sum[tile] = total[:, tile * 128:(tile + 1) * 128]
    start_all(scatter_col, 32)
    tile_parts[gy] = row_sum[mine]
    wait_all(scatter_col, 32)
    tile_total = tile_parts[0]
    for k in range(1, 32):
        tile_total = tile_total + tile_parts[k]
    tile_sum[mine] = tile_total
    start_all(gather_col, tiles)
    wait_all(gather_col, tiles)
    for tile in range(tiles):
        full[rows, tile * 128:(tile + 1) * 128] = tile_sum[tile]
    start_all(gather_row, 8)
    wait_all(gather_row, 8)
    o_ref[...] = full[...]


def add_up(table, collective_id):
    width = table.shape[1]
    tiles = width // 128
    dma = pltpu.SemaphoreType.DMA
    return pl.pallas_call(
        partial(add_up_kernel, tiles),
        out_shape=jax.ShapeDtypeStruct(table.shape, jnp.float32),
        in_specs=[pl.BlockSpec(memory_space=pltpu.VMEM)],
        out_specs=pl.BlockSpec(memory_space=pltpu.VMEM),
        scratch_shapes=[
            pltpu.VMEM((8, 8, width), jnp.float32),
            pltpu.VMEM((tiles, 8, 128), jnp.float32),
            pltpu.VMEM((32, 8, 128), jnp.float32),
            pltpu.VMEM((tiles, 8, 128), jnp.float32),
            pltpu.VMEM((64, width), jnp.float32),
            dma((8,)), dma((8,)), dma((32,)), dma((32,)), dma((tiles,)), dma((tiles,)), dma((8,)), dma((8,)),
        ],
        compiler_params=pltpu.CompilerParams(collective_id=collective_id, has_side_effects=True),
    )(table)


def passed_along(value, axis, steps):
    count = lax.axis_size(axis)
    leading, last = (max(0, -steps), min(count, count - steps))
    return lax.ppermute(value, axis, [(source, source + steps) for source in range(leading, last)])


def matmul(left_side, right_side):
    return jnp.dot(
        left_side, right_side, precision=lax.Precision.HIGHEST, preferred_element_type=jnp.float32
    )


def swish(values):
    return values * jax.nn.sigmoid(values)


def fine_update(
    latent, extended, edge_in, edge_out, node_in, node_out, edge_bias, node_bias, sources
):
    feature_count = latent.shape[0]
    receiver_part = matmul(edge_in[:, :feature_count], latent)
    sender_part = matmul(edge_in[:, feature_count:], extended)
    hidden = swish(receiver_part[:, None, :] + sender_part[:, sources] + edge_bias[:, None, None])
    summed = matmul(edge_out, jnp.sum(hidden, axis=1))
    activation = swish(
        matmul(node_in[:, :feature_count], latent)
        + matmul(node_in[:, feature_count:], summed)
        + node_bias[:, None]
    )
    return latent + matmul(node_out, activation)


def coarse_node(pooled, coarse_in, coarse_out, coarse_bias):
    return pooled + matmul(coarse_out, swish(matmul(coarse_in, pooled) + coarse_bias[:, None]))


def coarse_edge(nodes, coarse_mix, coarse_edges):
    gathered = nodes[:, coarse_edges[0]]
    summed = jnp.zeros_like(nodes).at[:, coarse_edges[1]].add(gathered)
    factor = (nodes.shape[1] / coarse_edges.shape[1]) ** 0.5
    return nodes + matmul(coarse_mix, summed) * factor


def up_update(middle, looked, up_in, up_out, up_bias):
    feature_count = middle.shape[0]
    activation = swish(
        matmul(up_in[:, :feature_count], middle)
        + matmul(up_in[:, feature_count:], looked)
        + up_bias[:, None]
    )
    return middle + matmul(up_out, activation)


def block_width(node_count):
    return math.gcd(node_count, 1024)


def one_hot_block(index_block, table_width):
    return (index_block[:, None] == jnp.arange(table_width, dtype=jnp.int32)[None, :]).astype(
        jnp.float32
    )


def pool_nodes(values, index, table_width):
    feature_count, node_count = values.shape
    width = block_width(node_count)
    blocks = node_count // width
    value_blocks = values.reshape(feature_count, blocks, width).transpose(1, 0, 2)
    index_blocks = index.reshape(blocks, width)

    def add_block(total, items):
        return (total + matmul(items[0], one_hot_block(items[1], table_width)), None)

    start = jnp.zeros((feature_count, table_width), jnp.float32)
    total, unused = lax.scan(add_block, start, (value_blocks, index_blocks))
    return total


def look_nodes(table, index):
    feature_count, table_width = table.shape
    node_count = index.shape[0]
    width = block_width(node_count)
    blocks = node_count // width
    index_blocks = index.reshape(blocks, width)

    def read_block(index_block):
        selector = one_hot_block(index_block, table_width)
        return lax.dot_general(
            table,
            selector,
            (((1,), (1,)), ((), ())),
            precision=lax.Precision.HIGHEST,
            preferred_element_type=jnp.float32,
        )

    result = lax.map(read_block, index_blocks)
    return result.transpose(1, 0, 2).reshape(feature_count, node_count)


def pass_rows(packet, offset):
    return passed_along(packet, "gx", offset)


def pass_cols(packet, offset):
    return passed_along(packet, "gy", offset)


def coarse_total(table):
    return add_up(table, 0)


def local(
    features,
    cotangent,
    edge_src,
    send_rows,
    fine_to_coarse,
    coarse_to_fine,
    coarse_edges,
    edge_in,
    edge_out,
    node_in,
    node_out,
    coarse_in,
    coarse_out,
    coarse_mix,
    up_in,
    up_out,
    biases,
):
    local_nodes = features.shape[1]
    halo_rows = send_rows.shape[1]
    pool_scale = (COARSE / (local_nodes * lax.axis_size("gx") * lax.axis_size("gy"))) ** 0.5
    packets = features[:, send_rows]
    extended = jnp.concatenate(
        [
            features,
            pass_rows(packets[:, 0], 1),
            pass_rows(packets[:, 1], -1),
            pass_cols(packets[:, 2], 1),
            pass_cols(packets[:, 3], -1),
        ],
        axis=1,
    )
    middle, fine_back = jax.vjp(
        partial(fine_update, sources=edge_src),
        features,
        extended,
        edge_in,
        edge_out,
        node_in,
        node_out,
        biases[0],
        biases[1],
    )
    pooled_part = pool_nodes(middle, fine_to_coarse, COARSE) * pool_scale
    pooled = coarse_total(pooled_part)
    nodes, node_back = jax.vjp(coarse_node, pooled, coarse_in, coarse_out, biases[2])
    mixed, mix_back = jax.vjp(partial(coarse_edge, coarse_edges=coarse_edges), nodes, coarse_mix)
    looked = look_nodes(mixed, coarse_to_fine)
    output, up_back = jax.vjp(up_update, middle, looked, up_in, up_out, biases[3])
    grad_middle, grad_looked, grad_up_in, grad_up_out, grad_up_bias = up_back(cotangent)
    grad_mixed_part = pool_nodes(grad_looked, coarse_to_fine, COARSE)
    grad_nodes_part, grad_mix = mix_back(grad_mixed_part)
    grad_nodes = coarse_total(grad_nodes_part)
    grad_pooled, grad_coarse_in, grad_coarse_out, grad_coarse_bias = node_back(grad_nodes)
    grad_middle = grad_middle + look_nodes(grad_pooled, fine_to_coarse) * pool_scale
    (
        grad_own,
        grad_ext,
        grad_edge_in,
        grad_edge_out,
        grad_node_in,
        grad_node_out,
        grad_edge_bias,
        grad_node_bias,
    ) = fine_back(grad_middle)
    pieces = [
        grad_ext[:, local_nodes + slot * halo_rows : local_nodes + (slot + 1) * halo_rows]
        for slot in range(4)
    ]
    returned = jnp.stack(
        [
            pass_rows(pieces[0], -1),
            pass_rows(pieces[1], 1),
            pass_cols(pieces[2], -1),
            pass_cols(pieces[3], 1),
        ],
        axis=1,
    )
    grad_features = (
        grad_own
        + grad_ext[:, :local_nodes]
        + jnp.zeros_like(features).at[:, send_rows].add(returned)
    )
    fine_biases = jnp.stack([grad_edge_bias, grad_node_bias, grad_up_bias])
    flat = jnp.concatenate([
        part.reshape(-1)
        for part in (grad_edge_in, grad_edge_out, grad_node_in, grad_node_out, grad_mix,
                     grad_up_in, grad_up_out, fine_biases)])
    count = flat.shape[0]
    whole = add_up(jnp.pad(flat, (0, 64 * 1024 - count)).reshape(64, 1024), 1).reshape(-1)
    shapes = ((64, 128), (64, 64), (64, 128), (64, 64), (64, 64), (64, 128), (64, 64), (3, 64))
    summed, offset = [], 0
    for shape in shapes:
        size = shape[0] * shape[1]
        summed.append(whole[offset:offset + size].reshape(shape))
        offset += size
    grad_biases = jnp.stack([summed[7][0], summed[7][1], grad_coarse_bias, summed[7][2]])
    return (
        output,
        grad_features,
        summed[0],
        summed[1],
        summed[2],
        summed[3],
        grad_coarse_in,
        grad_coarse_out,
        summed[4],
        summed[5],
        summed[6],
        grad_biases,
    )


def solution(mesh):
    in_specs = (
        P(None, ("gx", "gy")),
        P(None, ("gx", "gy")),
        P(None, ("gx", "gy")),
        P(None, ("gx", "gy")),
        P(("gx", "gy")),
        P(("gx", "gy")),
        P(),
        P(),
        P(),
        P(),
        P(),
        P(),
        P(),
        P(),
        P(),
        P(),
        P(),
    )
    out_specs = (
        P(None, ("gx", "gy")),
        P(None, ("gx", "gy")),
        P(),
        P(),
        P(),
        P(),
        P(),
        P(),
        P(),
        P(),
        P(),
        P(),
    )
    return jax.shard_map(local, mesh=mesh, in_specs=in_specs, out_specs=out_specs, check_vma=False)
```

```python
from functools import partial

import jax
import jax.numpy as jnp
from jax import lax
from jax.experimental import pallas as pl
from jax.experimental.pallas import tpu as pltpu
from jax.sharding import PartitionSpec as P

COARSE = 2048
EXT = 2560
RADIX = 256
SHIFT = 8
WIDTH = 2048
UNROLL = 1
VMEM_LIMIT = 56 * 2**20
PART = (16, 64, 128)
UPG = (2, 64, 128)
FG = (4, 64, 128)


def table_scratch():
    return ((EXT // RADIX * 64, 2 * RADIX), jnp.bfloat16)


def sums_scratch():
    return ((EXT // RADIX * 64, RADIX), jnp.float32)

MESH = pl.DeviceIdType.MESH


def halves(values):
    high = values.astype(jnp.bfloat16)
    return high, (values - high.astype(jnp.float32)).astype(jnp.bfloat16)


def product(left, right):
    left_high, left_low = halves(left)
    right_high, right_low = halves(right)
    return jnp.dot(jnp.concatenate([left_high, left_low, left_high], axis=1),
                   jnp.concatenate([right_high, right_high, right_low], axis=0),
                   preferred_element_type=jnp.float32)


def product_nt(left, right):
    left_high, left_low = halves(left)
    right_high, right_low = halves(right)
    return lax.dot_general(jnp.concatenate([left_high, left_low, left_high], axis=1),
                           jnp.concatenate([right_high, right_high, right_low], axis=1),
                           (((1,), (1,)), ((), ())), preferred_element_type=jnp.float32)


def product_tn(left, right):
    return product(left.T, right)


def selector(index_row):
    rows = lax.broadcasted_iota(jnp.int32, (RADIX, index_row.shape[1]), 0).astype(jnp.bfloat16)
    low = (index_row & (RADIX - 1)).astype(jnp.float32).astype(jnp.bfloat16)
    return jnp.where(rows == low, jnp.bfloat16(1), jnp.bfloat16(0))


def fill_table(table_ref, values):
    high, low = halves(values)
    for block in range(values.shape[1] // RADIX):
        columns = slice(block * RADIX, (block + 1) * RADIX)
        table_ref[block * 64:block * 64 + 64, :RADIX] = high[:, columns]
        table_ref[block * 64:block * 64 + 64, RADIX:] = low[:, columns]


def read_table(table_ref, blocks, index_row):
    picked = selector(index_row)
    found = jnp.dot(table_ref[:blocks * 64], jnp.concatenate([picked, picked], axis=0),
                    preferred_element_type=jnp.float32)
    chosen = jnp.broadcast_to(index_row >> SHIFT, (64, index_row.shape[1]))
    total = found[:64]
    for block in range(1, blocks):
        total = jnp.where(chosen == block, found[block * 64:block * 64 + 64], total)
    return total


def spread(values, blocks, index_row, low_column):
    high, low = halves(values)
    chosen = jnp.broadcast_to(index_row >> SHIFT, (64, index_row.shape[1]))
    parts = []
    for block in range(blocks):
        mask = jnp.where(chosen == block, 1.0, 0.0).astype(jnp.bfloat16)
        parts.append(jnp.concatenate([high * mask, low * mask], axis=1))
    lanes = lax.broadcasted_iota(jnp.int32, (low_column.shape[0], RADIX), 1).astype(jnp.bfloat16)
    picked = jnp.where(lanes == low_column.astype(jnp.bfloat16), jnp.bfloat16(1), jnp.bfloat16(0))
    return jnp.dot(jnp.concatenate(parts, axis=0), jnp.concatenate([picked, picked], axis=0),
                   preferred_element_type=jnp.float32)


def fill_columns(columns, rows):
    count = rows.shape[0]
    if count < 8:
        rows = jnp.concatenate([rows] * (8 // count), axis=0)
    turned = (rows & (RADIX - 1)).astype(jnp.float32).T
    for step in range(count):
        columns[step] = turned[:, step:step + 1]


def gathered_sums(sums_ref, blocks):
    return jnp.concatenate([sums_ref[block * 64:block * 64 + 64] for block in range(blocks)], axis=1)


def span(position, size):
    return pl.ds(pl.multiple_of(position * size, size), size)


def read_all(out_ref, table_ref, index_ref, width):
    def body(step, carry):
        part = span(step, width)
        out_ref[:, part] = read_table(table_ref, COARSE // RADIX, index_ref[:, part])
        return carry
    lax.fori_loop(0, index_ref.shape[1] // width, body, 0)


def spread_all(columns, values, index_row):
    blocks = COARSE // RADIX
    fill_columns(columns, index_row)
    found = spread(values, blocks, index_row, columns[0])
    return jnp.concatenate([found[block * 64:block * 64 + 64] for block in range(blocks)], axis=1)


def mix_all(sums_ref, table_ref, columns, edges_ref, sender, receiver):
    blocks = COARSE // RADIX
    sums_ref[:blocks * 64] = jnp.zeros((blocks * 64, RADIX), jnp.float32)
    fill_columns(columns, jnp.concatenate(
        [edges_ref[receiver:receiver + 1, step * 2048:step * 2048 + 2048] for step in range(4)], axis=0))

    def body(step, carry):
        part = span(step, 2048)
        found = read_table(table_ref, blocks, edges_ref[sender:sender + 1, part])
        sums_ref[:blocks * 64] += spread(found, blocks, edges_ref[receiver:receiver + 1, part], columns[step])
        return carry
    lax.fori_loop(0, 4, body, 0)
    return gathered_sums(sums_ref, blocks)


def extended(features, halo):
    return jnp.concatenate([features] + [halo[slot] for slot in range(4)], axis=1)


def put_slabs(out, values):
    for position in range(16):
        out[position] = values[:, position * 128:position * 128 + 128]


def gate(values):
    return 1.0 / (1.0 + jnp.exp(-values))


def silu_and_slope(values):
    opened = gate(values)
    silu = values * opened
    return silu, opened + silu * (1.0 - opened)


def fine_forward_kernel(scale, features, halo, sources, to_coarse, edge_in, edge_out, node_in, node_out, bias,
                        middle, slope, hidden, node_pre, pooled, table, received, sums, columns):
    feats = features[...]
    weights = edge_in[...]
    received[...] = product(weights[:, :64], feats) + bias[:, 0:1]
    fill_table(table, product(weights[:, 64:], extended(feats, halo)))

    def body(step, carry):
        part = span(step, WIDTH)
        base = received[:, part]

        def edge(k, total):
            silu, slopes = silu_and_slope(base + read_table(table, EXT // RADIX, sources[pl.ds(k, 1), part]))
            slope[k, :, part] = slopes
            return total + silu
        hidden[:, part] = lax.fori_loop(0, 8, edge, jnp.zeros((64, WIDTH), jnp.float32), unroll=UNROLL)
        return carry
    lax.fori_loop(0, 2048 // WIDTH, body, 0)
    aggregate = product(edge_out[...], hidden[...])
    pre = product(node_in[...], jnp.concatenate([feats, aggregate], axis=0)) + bias[:, 1:2]
    node_pre[...] = pre
    middle[...] = feats + product(node_out[...], pre * gate(pre))
    put_slabs(pooled, spread_all(columns, middle[...], to_coarse[...]) * scale)


def coarse_kernel(factor, pooled, coarse_in, coarse_out, coarse_mix, bias, edges, to_fine, middle, cotangent,
                  up_in, up_out, output, grad_middle, grad_mixed, mixed_sum, up_grads, table, looked, sums, columns):
    values = pooled[...]
    pre = product(coarse_in[...], values) + bias[:, 2:3]
    nodes = values + product(coarse_out[...], pre * gate(pre))
    fill_table(table, nodes)
    summed = mix_all(sums, table, columns, edges, 0, 1)
    mixed_sum[...] = summed
    fill_table(table, nodes + product(coarse_mix[...], summed) * factor)
    read_all(looked, table, to_fine, WIDTH)
    both = jnp.concatenate([middle[...], looked[...]], axis=0)
    silu, slopes = silu_and_slope(product(up_in[...], both) + bias[:, 3:4])
    output[...] = middle[...] + product(up_out[...], silu)
    cot = cotangent[...]
    grad_pre = product_tn(up_out[...], cot) * slopes
    up_grads[0] = product_nt(grad_pre, both)
    up_grads[1] = jnp.concatenate(
        [product_nt(cot, silu), jnp.broadcast_to(jnp.sum(grad_pre, axis=1, keepdims=True), (64, 64))], axis=1)
    grad_both = product_tn(up_in[...], grad_pre)
    grad_middle[...] = cot + grad_both[:64]
    put_slabs(grad_mixed, spread_all(columns, grad_both[64:], to_fine[...]))


def backward_kernel(factor, scale, grad_mixed, mixed_sum, pooled, coarse_in, coarse_out, coarse_mix, bias, edges,
                    to_coarse, grad_middle, node_pre, hidden, slope, features, halo, sources, edge_in, edge_out,
                    node_in, node_out, own, grad_halo, fine_grads, coarse_grads, table, found, scratch, sums, columns):
    grad_mix_all = grad_mixed[...]
    coarse_grads[:, 256:384] = jnp.concatenate(
        [product_nt(grad_mix_all, mixed_sum[...]) * factor, jnp.zeros((64, 64), jnp.float32)], axis=1)
    fill_table(table, product_tn(coarse_mix[...], grad_mix_all) * factor)
    grad_nodes = grad_mix_all + mix_all(sums, table, columns, edges, 1, 0)
    values = pooled[...]
    silu, slopes = silu_and_slope(product(coarse_in[...], values) + bias[:, 2:3])
    grad_pre = product_tn(coarse_out[...], grad_nodes) * slopes
    coarse_grads[:, 0:128] = jnp.concatenate([product_nt(grad_pre, values), product_nt(grad_nodes, silu)], axis=1)
    coarse_grads[:, 128:256] = jnp.broadcast_to(jnp.sum(grad_pre, axis=1, keepdims=True), (64, 128))
    fill_table(table, grad_nodes + product_tn(coarse_in[...], grad_pre))
    read_all(found, table, to_coarse, WIDTH)
    grad_mid = grad_middle[...] + found[...] * scale
    feats = features[...]
    silu, slopes = silu_and_slope(node_pre[...])
    aggregate = product(edge_out[...], hidden[...])
    grad_pre = product_tn(node_out[...], grad_mid) * slopes
    fine_grads[0] = product_nt(grad_pre, jnp.concatenate([feats, aggregate], axis=0))
    node_bias = jnp.sum(grad_pre, axis=1, keepdims=True)
    grad_both = product_tn(node_in[...], grad_pre)
    grad_sum = grad_both[64:]
    fine_grads[1] = jnp.concatenate(
        [product_nt(grad_mid, silu), product_nt(grad_sum, hidden[...])], axis=1)
    found[...] = grad_mid + grad_both[:64]
    scratch[...] = product_tn(edge_out[...], grad_sum)
    blocks = EXT // RADIX
    sums[...] = jnp.zeros(sums.shape, jnp.float32)
    fill_columns(columns, sources[...])

    def body(step, carry):
        part = span(step, WIDTH)
        base = scratch[:, part]

        def edge(k, total):
            grad_edge = base * slope[k, :, part]
            sums[...] += spread(grad_edge, blocks, sources[pl.ds(k, 1), part], columns[k, part])
            return total + grad_edge
        scratch[:, part] = lax.fori_loop(0, 8, edge, jnp.zeros((64, WIDTH), jnp.float32), unroll=UNROLL)
        return carry
    lax.fori_loop(0, 2048 // WIDTH, body, 0)
    grad_sent = gathered_sums(sums, blocks)
    grad_received = scratch[...]
    fine_grads[2] = jnp.concatenate(
        [product_nt(grad_received, feats),
         product_nt(grad_sent, extended(feats, halo))], axis=1)
    fine_grads[3] = jnp.concatenate(
        [jnp.broadcast_to(jnp.sum(grad_received, axis=1, keepdims=True), (64, 64)),
         jnp.broadcast_to(node_bias, (64, 64))], axis=1)
    weights = edge_in[...]
    back = product_tn(weights[:, 64:], grad_sent)
    own[...] = found[...] + product_tn(weights[:, :64], grad_received) + back[:, :2048]
    for slot in range(4):
        grad_halo[slot] = back[:, 2048 + slot * 128:2048 + slot * 128 + 128]


def call(kernel, outs, scratch, *operands):
    return pl.pallas_call(
        kernel,
        out_shape=[jax.ShapeDtypeStruct(shape, jnp.float32) for shape in outs],
        in_specs=[pl.BlockSpec(memory_space=pltpu.VMEM)] * len(operands),
        out_specs=[pl.BlockSpec(memory_space=pltpu.VMEM)] * len(outs),
        scratch_shapes=[pltpu.VMEM(shape, dtype) for shape, dtype in scratch],
        compiler_params=pltpu.CompilerParams(vmem_limit_bytes=VMEM_LIMIT),
    )(*operands)


def copy_to(source, target, sent, arrived, device):
    return pltpu.make_async_remote_copy(
        src_ref=source, dst_ref=target, send_sem=sent, recv_sem=arrived, device_id=device, device_id_type=MESH)


def each(make, count, action):
    def body(k, carry):
        getattr(make(k), action)()
        return carry
    lax.fori_loop(1, count, body, 0)


def side_devices(back):
    gx, gy = lax.axis_index("gx"), lax.axis_index("gy")
    up, down = (lax.rem(gx + 1, 8), gy), (lax.rem(gx + 7, 8), gy)
    right, left = (gx, lax.rem(gy + 1, 32)), (gx, lax.rem(gy + 31, 32))
    return (down, up, left, right) if back else (up, down, right, left)


def side_exists(back):
    gx, gy = lax.axis_index("gx"), lax.axis_index("gy")
    below = (gx > 0, gx < 7, gy > 0, gy < 31)
    return (below[1], below[0], below[3], below[2]) if back else below


def greet_sides(barrier):
    for device in side_devices(False):
        pl.semaphore_signal(barrier, inc=1, device_id=device, device_id_type=MESH)


class WholeSum:
    def __init__(self, slabs, x_ref, scratch):
        (self.half, self.core_parts, self.flat_parts, self.piece, self.line_parts, self.half_out, self.other,
         self.core_sems, self.flat_sent, self.flat_arrived, self.line_sent, self.line_arrived,
         self.back_sent, self.back_arrived) = scratch
        self.slabs, self.rows, self.x_ref = slabs, 2 * slabs, x_ref
        gx, gy = lax.axis_index("gx"), lax.axis_index("gy")
        self.core, self.z = lax.rem(gx, 2), lax.rem(gy, 8)
        self.flat = gx // 2 * 4 + gy // 8
        self.gx, self.gy = gx, gy
        self.sibling = (gx + 1 - 2 * self.core, gy)

    def flat_device(self, place):
        return (place // 4 * 2 + self.core, lax.rem(place, 4) * 8 + self.z)

    def line_device(self, z):
        return (self.gx, self.gy - self.z + z)

    def flat_place(self, k):
        return lax.rem(self.flat + k, 16)

    def chunk(self, ref, place):
        start = place * self.rows
        return ref.at[start // 32, pl.ds(pl.multiple_of(lax.rem(start, 32), 16), self.rows)]

    def own_rows(self, core):
        return pl.ds(pl.multiple_of(core * 32, 32), 32)

    def greet(self, barrier):
        pl.semaphore_signal(barrier, inc=1, device_id=self.sibling, device_id_type=MESH)

        def flat(k, carry):
            pl.semaphore_signal(barrier, inc=1, device_id=self.flat_device(self.flat_place(k)), device_id_type=MESH)
            return carry

        def line(k, carry):
            pl.semaphore_signal(barrier, inc=1, device_id=self.line_device(lax.rem(self.z + k, 8)),
                                device_id_type=MESH)
            return carry
        lax.fori_loop(1, 16, flat, 0)
        lax.fori_loop(1, 8, line, 0)
        return 23

    def to_core(self):
        return copy_to(self.x_ref.at[:, self.own_rows(1 - self.core)], self.core_parts,
                       self.core_sems.at[0], self.core_sems.at[1], self.sibling)

    def to_flat(self, k):
        place = self.flat_place(k)
        return copy_to(self.chunk(self.half, place), self.flat_parts.at[k], self.flat_sent.at[k],
                       self.flat_arrived.at[k], self.flat_device(place))

    def to_line(self, k):
        return copy_to(self.piece, self.line_parts.at[self.z], self.line_sent.at[k], self.line_arrived.at[k],
                       self.line_device(lax.rem(self.z + k, 8)))

    def back_flat(self, k):
        mine = self.chunk(self.half_out, self.flat)
        return copy_to(mine, mine, self.back_sent.at[k], self.back_arrived.at[k],
                       self.flat_device(self.flat_place(k)))

    def back_core(self):
        return copy_to(self.half_out, self.other, self.core_sems.at[2], self.core_sems.at[3], self.sibling)

    def run(self, beside=None):
        self.to_core().start()
        if beside is not None:
            beside()
        self.to_core().wait()
        self.half[...] = self.x_ref[:, self.own_rows(self.core)] + self.core_parts[...]
        each(self.to_flat, 16, "start")
        each(self.to_flat, 16, "wait")
        total = self.chunk(self.half, self.flat)[...]
        for k in range(1, 16):
            total = total + self.flat_parts[k]
        self.piece[...] = total
        each(self.to_line, 8, "start")
        self.line_parts[self.z] = total
        each(self.to_line, 8, "wait")
        total = self.line_parts[0]
        for k in range(1, 8):
            total = total + self.line_parts[k]
        self.chunk(self.half_out, self.flat)[...] = total
        each(self.back_flat, 16, "start")
        each(self.back_flat, 16, "wait")
        self.back_core().start()
        self.back_core().wait()

    def slab(self, position):
        first = jnp.broadcast_to(self.core == 0, (32, 128))
        own, other = self.half_out[position], self.other[position]
        return jnp.concatenate([jnp.where(first, own, other), jnp.where(first, other, own)], axis=0)


def sum_scratch(slabs):
    rows, dma = 2 * slabs, pltpu.SemaphoreType.DMA
    half = pltpu.VMEM((slabs, 32, 128), jnp.float32)
    return [half, half, pltpu.VMEM((16, rows, 128), jnp.float32), pltpu.VMEM((rows, 128), jnp.float32),
            pltpu.VMEM((8, rows, 128), jnp.float32), half, half,
            dma((4,)), dma((16,)), dma((16,)), dma((8,)), dma((8,)), dma((16,)), dma((16,))]


def remote_call(kernel, outs, scratch, collective_id, *operands):
    return pl.pallas_call(
        kernel,
        out_shape=[jax.ShapeDtypeStruct(shape, jnp.float32) for shape in outs],
        in_specs=[pl.BlockSpec(memory_space=pltpu.VMEM)] * len(operands),
        out_specs=[pl.BlockSpec(memory_space=pltpu.VMEM)] * len(outs),
        scratch_shapes=scratch,
        compiler_params=pltpu.CompilerParams(collective_id=collective_id, has_side_effects=True,
                                             vmem_limit_bytes=VMEM_LIMIT),
    )(*operands)


def add_up_kernel(x_ref, o_ref, *scratch):
    summing = WholeSum(16, x_ref, scratch)
    barrier = pltpu.get_barrier_semaphore()
    pl.semaphore_wait(barrier, summing.greet(barrier))
    summing.run()
    for position in range(16):
        o_ref[:, position * 128:position * 128 + 128] = summing.slab(position)


def add_up(table):
    total, = remote_call(add_up_kernel, [(64, 2048)], sum_scratch(16), 0, table)
    return total


def side_copy(packets, arrived_ref, sent, arrived, slot, back):
    return copy_to(packets.at[slot], arrived_ref.at[slot], sent.at[slot], arrived.at[slot], side_devices(back)[slot])


def halo_kernel(features, rows, halo, table, packets, arrived_ref, sent, arrived):
    barrier = pltpu.get_barrier_semaphore()
    greet_sides(barrier)
    fill_table(table, features[...])
    for slot in range(4):
        packets[slot] = read_table(table, COARSE // RADIX, rows[slot:slot + 1, :])
    pl.semaphore_wait(barrier, 4)
    for slot in range(4):
        side_copy(packets, arrived_ref, sent, arrived, slot, False).start()
    for slot in range(4):
        side_copy(packets, arrived_ref, sent, arrived, slot, False).wait()
        there = jnp.broadcast_to(side_exists(False)[slot], (64, 128))
        halo[slot] = jnp.where(there, arrived_ref[slot], 0.0)


def exchange(features, rows):
    dma = pltpu.SemaphoreType.DMA
    slots = pltpu.VMEM((4, 64, 128), jnp.float32)
    halo, = remote_call(
        halo_kernel, [(4, 64, 128)],
        [pltpu.VMEM((COARSE // RADIX * 64, 2 * RADIX), jnp.bfloat16), slots, slots, dma((4,)), dma((4,))],
        1, features, rows)
    return halo


def final_kernel(own, grad_halo, rows, fine_grads, up_grads, coarse_grads, grad_features, grad_edge_in,
                 grad_edge_out, grad_node_in, grad_node_out, grad_up_in, grad_up_out, grad_biases,
                 packed, arrived_ref, sent, arrived, *scratch):
    summing = WholeSum(8, packed, scratch)
    barrier = pltpu.get_barrier_semaphore()
    count = summing.greet(barrier)
    greet_sides(barrier)
    packed[0:4] = fine_grads[...]
    packed[4:6] = up_grads[...]
    packed[6:8] = jnp.zeros((2, 64, 128), jnp.float32)
    pl.semaphore_wait(barrier, count + 4)
    for slot in range(4):
        side_copy(grad_halo, arrived_ref, sent, arrived, slot, True).start()

    def add_returned():
        columns, parts = [], []
        for slot in range(4):
            side_copy(grad_halo, arrived_ref, sent, arrived, slot, True).wait()
            there = jnp.broadcast_to(side_exists(True)[slot], (64, 128))
            parts.append(jnp.where(there, arrived_ref[slot], 0.0))
        indices = rows[...]
        lows = (jnp.concatenate([indices, indices], axis=0) & (RADIX - 1)).astype(jnp.float32).T
        index_row = jnp.concatenate([indices[slot:slot + 1, :] for slot in range(4)], axis=1)
        low_column = jnp.concatenate([lows[:, slot:slot + 1] for slot in range(4)], axis=0)
        blocks = COARSE // RADIX
        found = spread(jnp.concatenate(parts, axis=1), blocks, index_row, low_column)
        for block in range(blocks):
            part = slice(block * RADIX, (block + 1) * RADIX)
            grad_features[:, part] = own[:, part] + found[block * 64:block * 64 + 64]
    summing.run(add_returned)
    grad_node_in[...] = summing.slab(0)
    pair = summing.slab(1)
    grad_node_out[...] = pair[:, :64]
    grad_edge_out[...] = pair[:, 64:]
    grad_edge_in[...] = summing.slab(2)
    grad_up_in[...] = summing.slab(4)
    last = summing.slab(5)
    grad_up_out[...] = last[:, :64]
    fine_bias, up_bias, coarse_bias = summing.slab(3).T, last.T, coarse_grads[:, 128:256].T
    grad_biases[...] = jnp.concatenate(
        [fine_bias[0:1], fine_bias[64:65], coarse_bias[0:1], up_bias[64:65]], axis=0)


def local(
    features,
    cotangent,
    edge_src,
    send_rows,
    fine_to_coarse,
    coarse_to_fine,
    coarse_edges,
    edge_in,
    edge_out,
    node_in,
    node_out,
    coarse_in,
    coarse_out,
    coarse_mix,
    up_in,
    up_out,
    biases,
):
    scale = (COARSE / (features.shape[1] * lax.axis_size("gx") * lax.axis_size("gy"))) ** 0.5
    factor = (COARSE / coarse_edges.shape[1]) ** 0.5
    bias = biases.T
    to_coarse, to_fine = fine_to_coarse.reshape(1, -1), coarse_to_fine.reshape(1, -1)
    table, sums, columns = table_scratch(), sums_scratch(), ((8, 2048, 1), jnp.float32)
    wide = ((64, 2048), jnp.float32)
    halo = exchange(features, send_rows)
    middle, slope, hidden, node_pre, pooled_part = call(
        partial(fine_forward_kernel, scale),
        [(64, 2048), (8, 64, 2048), (64, 2048), (64, 2048), PART],
        [table, wide, sums, columns],
        features, halo, edge_src, to_coarse, edge_in, edge_out, node_in, node_out, bias)
    pooled = add_up(pooled_part)
    output, grad_middle, grad_mixed_part, mixed_sum, up_grads = call(
        partial(coarse_kernel, factor),
        [(64, 2048), (64, 2048), PART, (64, 2048), UPG],
        [table, wide, sums, columns],
        pooled, coarse_in, coarse_out, coarse_mix, bias, coarse_edges, to_fine, middle, cotangent, up_in, up_out)
    grad_mixed = add_up(grad_mixed_part)
    own, grad_halo, fine_grads, coarse_grads = call(
        partial(backward_kernel, factor, scale),
        [(64, 2048), (4, 64, 128), FG, (64, 384)],
        [table, wide, wide, sums, columns],
        grad_mixed, mixed_sum, pooled, coarse_in, coarse_out, coarse_mix, bias, coarse_edges, to_coarse,
        grad_middle, node_pre, hidden, slope, features, halo, edge_src, edge_in, edge_out, node_in, node_out)
    dma = pltpu.SemaphoreType.DMA
    (grad_features, grad_edge_in, grad_edge_out, grad_node_in, grad_node_out, grad_up_in, grad_up_out,
     grad_biases) = remote_call(
        final_kernel,
        [(64, 2048), (64, 128), (64, 64), (64, 128), (64, 64), (64, 128), (64, 64), (4, 64)],
        [pltpu.VMEM((8, 64, 128), jnp.float32), pltpu.VMEM((4, 64, 128), jnp.float32), dma((4,)), dma((4,)),
         *sum_scratch(8)],
        2, own, grad_halo, send_rows, fine_grads, up_grads, coarse_grads)
    return (
        output,
        grad_features,
        grad_edge_in,
        grad_edge_out,
        grad_node_in,
        grad_node_out,
        coarse_grads[:, 0:64],
        coarse_grads[:, 64:128],
        coarse_grads[:, 256:320],
        grad_up_in,
        grad_up_out,
        grad_biases,
    )


def solution(mesh):
    in_specs = (
        P(None, ("gx", "gy")),
        P(None, ("gx", "gy")),
        P(None, ("gx", "gy")),
        P(None, ("gx", "gy")),
        P(("gx", "gy")),
        P(("gx", "gy")),
        P(),
        P(),
        P(),
        P(),
        P(),
        P(),
        P(),
        P(),
        P(),
        P(),
        P(),
    )
    out_specs = (
        P(None, ("gx", "gy")),
        P(None, ("gx", "gy")),
        P(),
        P(),
        P(),
        P(),
        P(),
        P(),
        P(),
        P(),
        P(),
        P(),
    )
    return jax.shard_map(local, mesh=mesh, in_specs=in_specs, out_specs=out_specs, check_vma=False)
```

```python
from functools import partial

import jax
import jax.numpy as jnp
from jax import lax
from jax.experimental import pallas as pl
from jax.experimental.pallas import tpu as pltpu
from jax.sharding import PartitionSpec as P

COARSE = 2048
EXT = 2560
RADIX = 256
SHIFT = 8
WIDTH = 2048
VMEM_LIMIT = 56 * 2**20


MESH = pl.DeviceIdType.MESH


def halves(values):
    high = values.astype(jnp.bfloat16)
    return high, (values - high.astype(jnp.float32)).astype(jnp.bfloat16)


def product(left, right):
    left_high, left_low = halves(left)
    right_high, right_low = halves(right)
    return jnp.dot(jnp.concatenate([left_high, left_low, left_high], axis=1),
                   jnp.concatenate([right_high, right_high, right_low], axis=0),
                   preferred_element_type=jnp.float32)


def product_nt(left, right):
    left_high, left_low = halves(left)
    right_high, right_low = halves(right)
    return lax.dot_general(jnp.concatenate([left_high, left_low, left_high], axis=1),
                           jnp.concatenate([right_high, right_high, right_low], axis=1),
                           (((1,), (1,)), ((), ())), preferred_element_type=jnp.float32)


def product_tn(left, right):
    return product(left.T, right)


def selector(index_row):
    rows = lax.broadcasted_iota(jnp.int32, (RADIX, index_row.shape[1]), 0).astype(jnp.bfloat16)
    low = (index_row & (RADIX - 1)).astype(jnp.float32).astype(jnp.bfloat16)
    return jnp.where(rows == low, jnp.bfloat16(1), jnp.bfloat16(0))


def fill_table(table_ref, values):
    high, low = halves(values)
    for block in range(values.shape[1] // RADIX):
        columns = slice(block * RADIX, (block + 1) * RADIX)
        rows = slice(block * values.shape[0], (block + 1) * values.shape[0])
        table_ref[rows, :RADIX] = high[:, columns]
        table_ref[rows, RADIX:] = low[:, columns]


def read_table(table_ref, blocks, index_row, height=64):
    picked = selector(index_row)
    found = jnp.dot(table_ref[:blocks * height], jnp.concatenate([picked, picked], axis=0),
                    preferred_element_type=jnp.float32)
    chosen = jnp.broadcast_to(index_row >> SHIFT, (height, index_row.shape[1]))
    total = found[:height]
    for block in range(1, blocks):
        total = jnp.where(chosen == block, found[block * height:(block + 1) * height], total)
    return total


def spread(values, blocks, index_row, low_column):
    high, low = halves(values)
    chosen = jnp.broadcast_to(index_row >> SHIFT, (values.shape[0], index_row.shape[1]))
    parts = []
    for block in range(blocks):
        mask = jnp.where(chosen == block, 1.0, 0.0).astype(jnp.bfloat16)
        parts.append(jnp.concatenate([high * mask, low * mask], axis=1))
    lanes = lax.broadcasted_iota(jnp.int32, (low_column.shape[0], RADIX), 1).astype(jnp.bfloat16)
    picked = jnp.where(lanes == low_column.astype(jnp.bfloat16), jnp.bfloat16(1), jnp.bfloat16(0))
    return jnp.dot(jnp.concatenate(parts, axis=0), jnp.concatenate([picked, picked], axis=0),
                   preferred_element_type=jnp.float32)


def fill_columns(columns, rows):
    count = rows.shape[0]
    if count < 8:
        rows = jnp.concatenate([rows] * (8 // count), axis=0)
    turned = (rows & (RADIX - 1)).astype(jnp.float32).T
    for step in range(count):
        columns[step] = turned[:, step:step + 1]


def gathered_sums(sums_ref, blocks, height=64):
    return jnp.concatenate(
        [sums_ref[block * height:(block + 1) * height] for block in range(blocks)], axis=1)


def span(position, size):
    return pl.ds(pl.multiple_of(position * size, size), size)


def read_all(out_ref, table_ref, index_ref, width):
    def body(step, carry):
        part = span(step, width)
        out_ref[:, part] = read_table(table_ref, COARSE // RADIX, index_ref[:, part])
        return carry
    lax.fori_loop(0, index_ref.shape[1] // width, body, 0)


def spread_all(columns, values, index_row):
    blocks = COARSE // RADIX
    fill_columns(columns, index_row)
    found = spread(values, blocks, index_row, columns[0])
    return jnp.concatenate([found[block * 64:block * 64 + 64] for block in range(blocks)], axis=1)


def mix_half(sums_ref, table_ref, columns, edges_ref, sender, receiver, values):
    blocks = COARSE // RADIX
    used = blocks * 32
    fill_table(table_ref, values)
    sums_ref[:used] = jnp.zeros((used, RADIX), jnp.float32)
    fill_columns(columns, jnp.concatenate(
        [edges_ref[receiver:receiver + 1, step * 2048:step * 2048 + 2048] for step in range(4)], axis=0))

    def body(step, carry):
        part = span(step, 2048)
        found = read_table(table_ref, blocks, edges_ref[sender:sender + 1, part], 32)
        sums_ref[:used] += spread(found, blocks, edges_ref[receiver:receiver + 1, part], columns[step])
        return carry
    lax.fori_loop(0, 4, body, 0)
    return gathered_sums(sums_ref, blocks, 32)


def bias_columns(biases):
    rows = biases[...]
    return jnp.concatenate([rows, rows], axis=0).T


def extended(features, halo):
    return jnp.concatenate([features] + [halo[slot] for slot in range(4)], axis=1)


def put_slabs(out, values):
    for position in range(16):
        out[position] = values[:, position * 128:position * 128 + 128]


def gate(values):
    return 1.0 / (1.0 + jnp.exp(-values))


def silu_and_slope(values):
    opened = gate(values)
    silu = values * opened
    return silu, opened + silu * (1.0 - opened)


def fine_forward_kernel(scale, features, halo, sources, to_coarse, edge_in, edge_out, node_in, node_out, biases,
                        middle, slope, hidden, node_pre, pooled, table, received, columns, packed, *scratch):
    summing = WholeSum(16, packed, scratch)
    barrier = pltpu.get_barrier_semaphore()
    count = summing.greet(barrier)
    bias = bias_columns(biases)
    feats = features[...]
    weights = edge_in[...]
    received[...] = product(weights[:, :64], feats) + bias[:, 0:1]
    fill_table(table, product(weights[:, 64:], extended(feats, halo)))

    def body(step, carry):
        part = span(step, WIDTH)
        base = received[:, part]

        def edge(k, total):
            silu, slopes = silu_and_slope(base + read_table(table, EXT // RADIX, sources[pl.ds(k, 1), part]))
            slope[k, :, part] = slopes
            return total + silu
        hidden[:, part] = lax.fori_loop(0, 8, edge, jnp.zeros((64, WIDTH), jnp.float32))
        return carry
    lax.fori_loop(0, 2048 // WIDTH, body, 0)
    aggregate = product(edge_out[...], hidden[...])
    pre = product(node_in[...], jnp.concatenate([feats, aggregate], axis=0)) + bias[:, 1:2]
    node_pre[...] = pre
    middle[...] = feats + product(node_out[...], pre * gate(pre))
    put_slabs(packed, spread_all(columns, middle[...], to_coarse[...]) * scale)
    pl.semaphore_wait(barrier, count)
    summing.run()
    for position in range(16):
        pooled[:, position * 128:position * 128 + 128] = summing.slab(position)


def coarse_kernel(factor, pooled, coarse_in, coarse_out, coarse_mix, biases, edges, to_fine, middle, cotangent,
                  up_in, up_out, output, grad_middle, grad_mixed, mixed_back, mixed_sum, up_grads, table, looked,
                  sums, columns, packed, mine, theirs, mine_back, theirs_back, swap_sems, *scratch):
    summing = WholeSum(16, packed, scratch)
    barrier = pltpu.get_barrier_semaphore()
    count = summing.greet(barrier)
    bias = bias_columns(biases)
    first = jnp.broadcast_to(summing.core == 0, (32, 2048))
    values = pooled[...]
    pre = product(coarse_in[...], values) + bias[:, 2:3]
    nodes = values + product(coarse_out[...], pre * gate(pre))
    mine[...] = mix_half(sums, table, columns, edges, 0, 1, jnp.where(first, nodes[:32], nodes[32:]))
    pl.semaphore_wait(barrier, count)
    swap = copy_to(mine, theirs, swap_sems.at[0], swap_sems.at[1], summing.sibling)
    swap.start()
    swap.wait()
    summed = jnp.concatenate([jnp.where(first, mine[...], theirs[...]), jnp.where(first, theirs[...], mine[...])],
                             axis=0)
    mixed_sum[...] = summed
    fill_table(table, nodes + product(coarse_mix[...], summed) * factor)
    read_all(looked, table, to_fine, WIDTH)
    both = jnp.concatenate([middle[...], looked[...]], axis=0)
    silu, slopes = silu_and_slope(product(up_in[...], both) + bias[:, 3:4])
    output[...] = middle[...] + product(up_out[...], silu)
    cot = cotangent[...]
    grad_pre = product_tn(up_out[...], cot) * slopes
    up_grads[0] = product_nt(grad_pre, both)
    up_grads[1] = jnp.concatenate(
        [product_nt(cot, silu), jnp.broadcast_to(jnp.sum(grad_pre, axis=1, keepdims=True), (64, 64))], axis=1)
    grad_both = product_tn(up_in[...], grad_pre)
    grad_middle[...] = cot + grad_both[:64]
    put_slabs(packed, spread_all(columns, grad_both[64:], to_fine[...]))
    summing.run(back=False)
    summing.back_core().start()
    own_half = jnp.concatenate([summing.half_out[position] for position in range(16)], axis=1)
    mine_back[...] = mix_half(sums, table, columns, edges, 1, 0, own_half)
    swap = copy_to(mine_back, theirs_back, swap_sems.at[2], swap_sems.at[3], summing.sibling)
    swap.start()
    summing.back_core().wait()
    for position in range(16):
        grad_mixed[:, position * 128:position * 128 + 128] = summing.slab(position)
    swap.wait()
    mixed_back[:32] = jnp.where(first, mine_back[...], theirs_back[...])
    mixed_back[32:] = jnp.where(first, theirs_back[...], mine_back[...])


def backward_kernel(factor, scale, grad_mixed, mixed_back, mixed_sum, pooled, coarse_in, coarse_out, coarse_mix,
                    biases, to_coarse, grad_middle, node_pre, hidden, slope, features, halo, sources, edge_in,
                    edge_out, node_in, node_out, up_grads, rows, grad_features, weight_sums, coarse_grads, table,
                    found, scratch, sums, columns, own, grad_halo, packed, arrived_ref, sent, arrived, *sum_refs):
    summing = WholeSum(8, packed, sum_refs)
    barrier = pltpu.get_barrier_semaphore()
    count = summing.greet(barrier)
    greet_sides(barrier)
    bias = bias_columns(biases)
    packed[4:6] = up_grads[...]
    packed[6:8] = jnp.zeros((2, 64, 128), jnp.float32)
    grad_mix_all = grad_mixed[...]
    coarse_grads[:, 256:384] = jnp.concatenate(
        [product_nt(grad_mix_all, mixed_sum[...]) * factor, jnp.zeros((64, 64), jnp.float32)], axis=1)
    grad_nodes = grad_mix_all + product_tn(coarse_mix[...], mixed_back[...]) * factor
    values = pooled[...]
    silu, slopes = silu_and_slope(product(coarse_in[...], values) + bias[:, 2:3])
    grad_pre = product_tn(coarse_out[...], grad_nodes) * slopes
    coarse_grads[:, 0:128] = jnp.concatenate([product_nt(grad_pre, values), product_nt(grad_nodes, silu)], axis=1)
    coarse_grads[:, 128:256] = jnp.broadcast_to(jnp.sum(grad_pre, axis=1, keepdims=True), (64, 128))
    fill_table(table, grad_nodes + product_tn(coarse_in[...], grad_pre))
    read_all(found, table, to_coarse, WIDTH)
    grad_mid = grad_middle[...] + found[...] * scale
    feats = features[...]
    silu, slopes = silu_and_slope(node_pre[...])
    aggregate = product(edge_out[...], hidden[...])
    grad_pre = product_tn(node_out[...], grad_mid) * slopes
    packed[0] = product_nt(grad_pre, jnp.concatenate([feats, aggregate], axis=0))
    node_bias = jnp.sum(grad_pre, axis=1, keepdims=True)
    grad_both = product_tn(node_in[...], grad_pre)
    grad_sum = grad_both[64:]
    packed[1] = jnp.concatenate(
        [product_nt(grad_mid, silu), product_nt(grad_sum, hidden[...])], axis=1)
    found[...] = grad_mid + grad_both[:64]
    scratch[...] = product_tn(edge_out[...], grad_sum)
    blocks = EXT // RADIX
    sums[...] = jnp.zeros(sums.shape, jnp.float32)
    fill_columns(columns, sources[...])

    def body(step, carry):
        part = span(step, WIDTH)
        base = scratch[:, part]

        def edge(k, total):
            grad_edge = base * slope[k, :, part]
            sums[...] += spread(grad_edge, blocks, sources[pl.ds(k, 1), part], columns[k, part])
            return total + grad_edge
        scratch[:, part] = lax.fori_loop(0, 8, edge, jnp.zeros((64, WIDTH), jnp.float32))
        return carry
    lax.fori_loop(0, 2048 // WIDTH, body, 0)
    grad_sent = gathered_sums(sums, blocks)
    grad_received = scratch[...]
    packed[2] = jnp.concatenate(
        [product_nt(grad_received, feats),
         product_nt(grad_sent, extended(feats, halo))], axis=1)
    packed[3] = jnp.concatenate(
        [jnp.broadcast_to(jnp.sum(grad_received, axis=1, keepdims=True), (64, 64)),
         jnp.broadcast_to(node_bias, (64, 64))], axis=1)
    weights = edge_in[...]
    back = product_tn(weights[:, 64:], grad_sent)
    own[...] = found[...] + product_tn(weights[:, :64], grad_received) + back[:, :2048]
    for slot in range(4):
        grad_halo[slot] = back[:, 2048 + slot * 128:2048 + slot * 128 + 128]
    pl.semaphore_wait(barrier, count + 4)
    for slot in range(4):
        side_copy(grad_halo, arrived_ref, sent, arrived, slot, True).start()

    def add_returned():
        columns, parts = [], []
        for slot in range(4):
            side_copy(grad_halo, arrived_ref, sent, arrived, slot, True).wait()
            there = jnp.broadcast_to(side_exists(True)[slot], (64, 128))
            parts.append(jnp.where(there, arrived_ref[slot], 0.0))
        indices = rows[...]
        lows = (jnp.concatenate([indices, indices], axis=0) & (RADIX - 1)).astype(jnp.float32).T
        index_row = jnp.concatenate([indices[slot:slot + 1, :] for slot in range(4)], axis=1)
        low_column = jnp.concatenate([lows[:, slot:slot + 1] for slot in range(4)], axis=0)
        blocks = COARSE // RADIX
        found = spread(jnp.concatenate(parts, axis=1), blocks, index_row, low_column)
        for block in range(blocks):
            part = slice(block * RADIX, (block + 1) * RADIX)
            grad_features[:, part] = own[:, part] + found[block * 64:block * 64 + 64]
    summing.run(add_returned)
    for position in range(8):
        weight_sums[position] = summing.slab(position)


def call(kernel, outs, scratch, *operands):
    return pl.pallas_call(
        kernel,
        out_shape=[jax.ShapeDtypeStruct(shape, jnp.float32) for shape in outs],
        in_specs=[pl.BlockSpec(memory_space=pltpu.VMEM)] * len(operands),
        out_specs=[pl.BlockSpec(memory_space=pltpu.VMEM)] * len(outs),
        scratch_shapes=[pltpu.VMEM(shape, dtype) for shape, dtype in scratch],
        compiler_params=pltpu.CompilerParams(vmem_limit_bytes=VMEM_LIMIT),
    )(*operands)


def copy_to(source, target, sent, arrived, device):
    return pltpu.make_async_remote_copy(
        src_ref=source, dst_ref=target, send_sem=sent, recv_sem=arrived, device_id=device, device_id_type=MESH)


def each(make, count):
    for k in range(1, count):
        make(k).start()
    for k in range(1, count):
        make(k).wait()


def turned(place, count):
    return jnp.where(place >= count, place - count, place)


def side_devices(back):
    gx, gy = lax.axis_index("gx"), lax.axis_index("gy")
    up, down = (lax.rem(gx + 1, 8), gy), (lax.rem(gx + 7, 8), gy)
    right, left = (gx, lax.rem(gy + 1, 32)), (gx, lax.rem(gy + 31, 32))
    return (down, up, left, right) if back else (up, down, right, left)


def side_exists(back):
    gx, gy = lax.axis_index("gx"), lax.axis_index("gy")
    below = (gx > 0, gx < 7, gy > 0, gy < 31)
    return (below[1], below[0], below[3], below[2]) if back else below


def greet_sides(barrier):
    for device in side_devices(False):
        pl.semaphore_signal(barrier, inc=1, device_id=device, device_id_type=MESH)


class WholeSum:
    def __init__(self, slabs, x_ref, scratch):
        (self.half, self.core_parts, self.flat_parts, self.piece, self.line_parts, self.half_out, self.other,
         self.core_sems, self.flat_sent, self.flat_arrived, self.line_sent, self.line_arrived,
         self.back_sent, self.back_arrived) = scratch
        self.slabs, self.rows, self.x_ref = slabs, 2 * slabs, x_ref
        gx, gy = lax.axis_index("gx"), lax.axis_index("gy")
        self.x, self.y = gx // 2, gy // 8
        self.core, self.z = gx - 2 * self.x, gy - 8 * self.y
        self.gx, self.gy = gx, gy
        self.sibling = (gx + 1 - 2 * self.core, gy)
        self.xs = [turned(self.x + k, 4) for k in range(4)]
        self.ys = [turned(self.y + k, 4) for k in range(4)]
        self.zs = [turned(self.z + k, 8) for k in range(8)]

    def flat_device(self, k):
        return (self.xs[k // 4] * 2 + self.core, self.ys[k % 4] * 8 + self.z)

    def line_device(self, k):
        return (self.gx, self.y * 8 + self.zs[k])

    def chunk(self, ref, k):
        x, y = self.xs[k // 4], self.ys[k % 4]
        if self.rows == 32:
            return ref.at[x * 4 + y]
        high = y // 2
        return ref.at[x * 2 + high, pl.ds(pl.multiple_of((y - 2 * high) * 16, 16), 16)]

    def own_rows(self, core):
        return pl.ds(pl.multiple_of(core * 32, 32), 32)

    def greet(self, barrier):
        devices = ([self.sibling] + [self.line_device(k) for k in range(1, 8)]
                   + [self.flat_device(k) for k in range(1, 16)])
        for device in devices:
            pl.semaphore_signal(barrier, inc=1, device_id=device, device_id_type=MESH)
        return len(devices)

    def to_core(self):
        return copy_to(self.x_ref.at[:, self.own_rows(1 - self.core)], self.core_parts,
                       self.core_sems.at[0], self.core_sems.at[1], self.sibling)

    def to_flat(self, k):
        return copy_to(self.chunk(self.half, k), self.flat_parts.at[k], self.flat_sent.at[k],
                       self.flat_arrived.at[k], self.flat_device(k))

    def to_line(self, k):
        return copy_to(self.piece, self.line_parts.at[self.z], self.line_sent.at[k], self.line_arrived.at[k],
                       self.line_device(k))

    def back_flat(self, k):
        mine = self.chunk(self.half_out, 0)
        return copy_to(mine, mine, self.back_sent.at[k], self.back_arrived.at[k], self.flat_device(k))

    def back_core(self):
        return copy_to(self.half_out, self.other, self.core_sems.at[2], self.core_sems.at[3], self.sibling)

    def run(self, beside=None, back=True):
        self.to_core().start()
        if beside is not None:
            beside()
        self.to_core().wait()
        self.half[...] = self.x_ref[:, self.own_rows(self.core)] + self.core_parts[...]
        each(self.to_flat, 16)
        total = self.chunk(self.half, 0)[...]
        for k in range(1, 16):
            total = total + self.flat_parts[k]
        self.piece[...] = total
        self.line_parts[self.z] = total
        each(self.to_line, 8)
        total = self.line_parts[0]
        for k in range(1, 8):
            total = total + self.line_parts[k]
        self.chunk(self.half_out, 0)[...] = total
        each(self.back_flat, 16)
        if back:
            self.back_core().start()
            self.back_core().wait()

    def slab(self, position):
        first = jnp.broadcast_to(self.core == 0, (32, 128))
        own, other = self.half_out[position], self.other[position]
        return jnp.concatenate([jnp.where(first, own, other), jnp.where(first, other, own)], axis=0)


def sum_scratch(slabs):
    rows, dma = 2 * slabs, pltpu.SemaphoreType.DMA
    half = pltpu.VMEM((slabs, 32, 128), jnp.float32)
    return [half, half, pltpu.VMEM((16, rows, 128), jnp.float32), pltpu.VMEM((rows, 128), jnp.float32),
            pltpu.VMEM((8, rows, 128), jnp.float32), half, half,
            dma((4,)), dma((16,)), dma((16,)), dma((8,)), dma((8,)), dma((16,)), dma((16,))]


def remote_call(kernel, outs, scratch, collective_id, *operands):
    return pl.pallas_call(
        kernel,
        out_shape=[jax.ShapeDtypeStruct(shape, jnp.float32) for shape in outs],
        in_specs=[pl.BlockSpec(memory_space=pltpu.VMEM)] * len(operands),
        out_specs=[pl.BlockSpec(memory_space=pltpu.VMEM)] * len(outs),
        scratch_shapes=scratch,
        compiler_params=pltpu.CompilerParams(collective_id=collective_id, has_side_effects=True,
                                             vmem_limit_bytes=VMEM_LIMIT),
    )(*operands)


def side_copy(packets, arrived_ref, sent, arrived, slot, back):
    return copy_to(packets.at[slot], arrived_ref.at[slot], sent.at[slot], arrived.at[slot], side_devices(back)[slot])


def halo_kernel(features, rows, halo, table, packets, arrived_ref, sent, arrived):
    barrier = pltpu.get_barrier_semaphore()
    greet_sides(barrier)
    fill_table(table, features[...])
    for slot in range(4):
        packets[slot] = read_table(table, COARSE // RADIX, rows[slot:slot + 1, :])
    pl.semaphore_wait(barrier, 4)
    for slot in range(4):
        side_copy(packets, arrived_ref, sent, arrived, slot, False).start()
    for slot in range(4):
        side_copy(packets, arrived_ref, sent, arrived, slot, False).wait()
        there = jnp.broadcast_to(side_exists(False)[slot], (64, 128))
        halo[slot] = jnp.where(there, arrived_ref[slot], 0.0)


def exchange(features, rows):
    dma = pltpu.SemaphoreType.DMA
    slots = pltpu.VMEM((4, 64, 128), jnp.float32)
    halo, = remote_call(
        halo_kernel, [(4, 64, 128)],
        [pltpu.VMEM((COARSE // RADIX * 64, 2 * RADIX), jnp.bfloat16), slots, slots, dma((4,)), dma((4,))],
        1, features, rows)
    return halo


def unpack_kernel(output, grad_features, weight_sums, coarse_grads, out, out_features, grad_edge_in, grad_edge_out,
                  grad_node_in, grad_node_out, grad_coarse_in, grad_coarse_out, grad_coarse_mix, grad_up_in,
                  grad_up_out, grad_biases):
    out[...] = output[...]
    out_features[...] = grad_features[...]
    grad_node_in[...] = weight_sums[0]
    pair = weight_sums[1]
    grad_node_out[...] = pair[:, :64]
    grad_edge_out[...] = pair[:, 64:]
    grad_edge_in[...] = weight_sums[2]
    grad_up_in[...] = weight_sums[4]
    last = weight_sums[5]
    grad_up_out[...] = last[:, :64]
    grad_coarse_in[...] = coarse_grads[:, 0:64]
    grad_coarse_out[...] = coarse_grads[:, 64:128]
    grad_coarse_mix[...] = coarse_grads[:, 256:320]
    fine_bias, up_bias, coarse_bias = weight_sums[3].T, last.T, coarse_grads[:, 128:256].T
    grad_biases[...] = jnp.concatenate(
        [fine_bias[0:1], fine_bias[64:65], coarse_bias[0:1], up_bias[64:65]], axis=0)


def local(
    features,
    cotangent,
    edge_src,
    send_rows,
    fine_to_coarse,
    coarse_to_fine,
    coarse_edges,
    edge_in,
    edge_out,
    node_in,
    node_out,
    coarse_in,
    coarse_out,
    coarse_mix,
    up_in,
    up_out,
    biases,
):
    scale = (COARSE / (features.shape[1] * lax.axis_size("gx") * lax.axis_size("gy"))) ** 0.5
    factor = (COARSE / coarse_edges.shape[1]) ** 0.5
    f32, dma = jnp.float32, pltpu.SemaphoreType.DMA
    to_coarse, to_fine = fine_to_coarse.reshape(1, -1), coarse_to_fine.reshape(1, -1)
    table = pltpu.VMEM((EXT // RADIX * 64, 2 * RADIX), jnp.bfloat16)
    sums, columns = pltpu.VMEM((EXT // RADIX * 64, RADIX), f32), pltpu.VMEM((8, 2048, 1), f32)
    wide, half = pltpu.VMEM((64, 2048), f32), pltpu.VMEM((32, 2048), f32)
    slots = pltpu.VMEM((4, 64, 128), f32)
    halo = exchange(features, send_rows)
    middle, slope, hidden, node_pre, pooled = remote_call(
        partial(fine_forward_kernel, scale),
        [(64, 2048), (8, 64, 2048), (64, 2048), (64, 2048), (64, 2048)],
        [table, wide, columns, pltpu.VMEM((16, 64, 128), f32), *sum_scratch(16)], 2,
        features, halo, edge_src, to_coarse, edge_in, edge_out, node_in, node_out, biases)
    output, grad_middle, grad_mixed, mixed_back, mixed_sum, up_grads = remote_call(
        partial(coarse_kernel, factor),
        [(64, 2048), (64, 2048), (64, 2048), (64, 2048), (64, 2048), (2, 64, 128)],
        [table, wide, sums, columns, pltpu.VMEM((16, 64, 128), f32), half, half, half, half, dma((4,)),
         *sum_scratch(16)], 3,
        pooled, coarse_in, coarse_out, coarse_mix, biases, coarse_edges, to_fine, middle, cotangent, up_in, up_out)
    grad_features, weight_sums, coarse_grads = remote_call(
        partial(backward_kernel, factor, scale),
        [(64, 2048), (8, 64, 128), (64, 384)],
        [table, wide, wide, sums, columns, wide, slots, pltpu.VMEM((8, 64, 128), f32), slots, dma((4,)), dma((4,)),
         *sum_scratch(8)], 4,
        grad_mixed, mixed_back, mixed_sum, pooled, coarse_in, coarse_out, coarse_mix, biases, to_coarse,
        grad_middle, node_pre, hidden, slope, features, halo, edge_src, edge_in, edge_out, node_in, node_out,
        up_grads, send_rows)
    (out, out_features, grad_edge_in, grad_edge_out, grad_node_in, grad_node_out, grad_coarse_in, grad_coarse_out,
     grad_coarse_mix, grad_up_in, grad_up_out, grad_biases) = call(
        unpack_kernel,
        [(64, 2048), (64, 2048), (64, 128), (64, 64), (64, 128), (64, 64), (64, 64), (64, 64), (64, 64), (64, 128),
         (64, 64), (4, 64)], [], output, grad_features, weight_sums, coarse_grads)
    return (out, out_features, grad_edge_in, grad_edge_out, grad_node_in, grad_node_out, grad_coarse_in,
            grad_coarse_out, grad_coarse_mix, grad_up_in, grad_up_out, grad_biases)


def solution(mesh):
    in_specs = (
        P(None, ("gx", "gy")),
        P(None, ("gx", "gy")),
        P(None, ("gx", "gy")),
        P(None, ("gx", "gy")),
        P(("gx", "gy")),
        P(("gx", "gy")),
        P(),
        P(),
        P(),
        P(),
        P(),
        P(),
        P(),
        P(),
        P(),
        P(),
        P(),
    )
    out_specs = (
        P(None, ("gx", "gy")),
        P(None, ("gx", "gy")),
        P(),
        P(),
        P(),
        P(),
        P(),
        P(),
        P(),
        P(),
        P(),
        P(),
    )
    return jax.shard_map(local, mesh=mesh, in_specs=in_specs, out_specs=out_specs, check_vma=False)
```

```python
from functools import partial

import jax
import jax.numpy as jnp
from jax import lax
from jax.experimental import pallas as pl
from jax.experimental.pallas import tpu as pltpu
from jax.sharding import PartitionSpec as P

COARSE = 2048
EXT = 2560
RADIX = 256
SHIFT = 8
WIDTH = 2048
VMEM_LIMIT = 56 * 2**20


MESH = pl.DeviceIdType.MESH


def halves(values):
    high = values.astype(jnp.bfloat16)
    return high, (values - high.astype(jnp.float32)).astype(jnp.bfloat16)


def product(left, right):
    left_high, left_low = halves(left)
    right_high, right_low = halves(right)
    return jnp.dot(jnp.concatenate([left_high, left_low, left_high], axis=1),
                   jnp.concatenate([right_high, right_high, right_low], axis=0),
                   preferred_element_type=jnp.float32)


def product_nt(left, right):
    left_high, left_low = halves(left)
    right_high, right_low = halves(right)
    return lax.dot_general(jnp.concatenate([left_high, left_low, left_high], axis=1),
                           jnp.concatenate([right_high, right_high, right_low], axis=1),
                           (((1,), (1,)), ((), ())), preferred_element_type=jnp.float32)


def product_tn(left, right):
    return product(left.T, right)


def selector(index_row):
    rows = lax.broadcasted_iota(jnp.int32, (RADIX, index_row.shape[1]), 0).astype(jnp.bfloat16)
    low = (index_row & (RADIX - 1)).astype(jnp.float32).astype(jnp.bfloat16)
    return jnp.where(rows == low, jnp.bfloat16(1), jnp.bfloat16(0))


def fill_table(table_ref, values):
    high, low = halves(values)
    for block in range(values.shape[1] // RADIX):
        columns = slice(block * RADIX, (block + 1) * RADIX)
        rows = slice(block * values.shape[0], (block + 1) * values.shape[0])
        table_ref[rows, :RADIX] = high[:, columns]
        table_ref[rows, RADIX:] = low[:, columns]


def read_table(table_ref, blocks, index_row, height=64):
    picked = selector(index_row)
    found = jnp.dot(table_ref[:blocks * height], jnp.concatenate([picked, picked], axis=0),
                    preferred_element_type=jnp.float32)
    chosen = jnp.broadcast_to(index_row >> SHIFT, (height, index_row.shape[1]))
    total = found[:height]
    for block in range(1, blocks):
        total = jnp.where(chosen == block, found[block * height:(block + 1) * height], total)
    return total


def lane_gather(table_ref, first, index_row, start):
    pieces = []
    for piece in range(index_row.shape[1] // 128):
        row = index_row[:, piece * 128:piece * 128 + 128]
        lanes = jnp.broadcast_to(row & 127, (64, 128))
        chosen = jnp.broadcast_to(row >> 7, (64, 128))
        total = start[:, piece * 128:piece * 128 + 128]
        for block in range(table_ref.shape[1] // 128):
            found = jnp.take_along_axis(table_ref[:, block * 128:block * 128 + 128], lanes, axis=1)
            total = jnp.where(chosen == first + block, found, total)
        pieces.append(total)
    return jnp.concatenate(pieces, axis=1)


def spread(values, blocks, index_row, low_column):
    high, low = halves(values)
    chosen = jnp.broadcast_to(index_row >> SHIFT, (values.shape[0], index_row.shape[1]))
    parts = []
    for block in range(blocks):
        mask = jnp.where(chosen == block, 1.0, 0.0).astype(jnp.bfloat16)
        parts.append(jnp.concatenate([high * mask, low * mask], axis=1))
    lanes = lax.broadcasted_iota(jnp.int32, (low_column.shape[0], RADIX), 1).astype(jnp.bfloat16)
    picked = jnp.where(lanes == low_column.astype(jnp.bfloat16), jnp.bfloat16(1), jnp.bfloat16(0))
    return jnp.dot(jnp.concatenate(parts, axis=0), jnp.concatenate([picked, picked], axis=0),
                   preferred_element_type=jnp.float32)


def fill_columns(columns, rows):
    count = rows.shape[0]
    if count < 8:
        rows = jnp.concatenate([rows] * (8 // count), axis=0)
    turned = (rows & (RADIX - 1)).astype(jnp.float32).T
    for step in range(count):
        columns[step] = turned[:, step:step + 1]


def gathered_sums(sums_ref, blocks, height=64):
    return jnp.concatenate(
        [sums_ref[block * height:(block + 1) * height] for block in range(blocks)], axis=1)


def span(position, size):
    return pl.ds(pl.multiple_of(position * size, size), size)


def read_all(out_ref, table_ref, index_ref, width):
    def body(step, carry):
        part = span(step, width)
        out_ref[:, part] = read_table(table_ref, COARSE // RADIX, index_ref[:, part])
        return carry
    lax.fori_loop(0, index_ref.shape[1] // width, body, 0)


def spread_all(columns, values, index_row):
    blocks = COARSE // RADIX
    fill_columns(columns, index_row)
    found = spread(values, blocks, index_row, columns[0])
    return jnp.concatenate([found[block * 64:block * 64 + 64] for block in range(blocks)], axis=1)


def mix_half(sums_ref, table_ref, columns, edges_ref, sender, receiver, values):
    blocks = COARSE // RADIX
    used = blocks * 32
    fill_table(table_ref, values)
    sums_ref[:used] = jnp.zeros((used, RADIX), jnp.float32)
    fill_columns(columns, jnp.concatenate(
        [edges_ref[receiver:receiver + 1, step * 2048:step * 2048 + 2048] for step in range(4)], axis=0))

    def body(step, carry):
        part = span(step, 2048)
        found = read_table(table_ref, blocks, edges_ref[sender:sender + 1, part], 32)
        sums_ref[:used] += spread(found, blocks, edges_ref[receiver:receiver + 1, part], columns[step])
        return carry
    lax.fori_loop(0, 4, body, 0, unroll=4)
    return gathered_sums(sums_ref, blocks, 32)


def bias_columns(biases):
    rows = biases[...]
    return jnp.concatenate([rows, rows], axis=0).T


def extended(features, halo):
    return jnp.concatenate([features] + [halo[slot] for slot in range(4)], axis=1)


def put_slabs(out, values):
    for position in range(16):
        out[position] = values[:, position * 128:position * 128 + 128]


def gate(values):
    return 1.0 / (1.0 + jnp.exp(-values))


def silu_and_slope(values):
    opened = gate(values)
    silu = values * opened
    return silu, opened + silu * (1.0 - opened)


def fine_forward_kernel(scale, features, halo, sources, to_coarse, edge_in, edge_out, node_in, node_out, biases,
                        middle, slope, hidden, node_pre, pooled, table, received, columns, packed, tail, *scratch):
    summing = WholeSum(16, packed, scratch)
    barrier = pltpu.get_barrier_semaphore()
    count = summing.greet(barrier)
    bias = bias_columns(biases)
    feats = features[...]
    weights = edge_in[...]
    received[...] = product(weights[:, :64], feats) + bias[:, 0:1]
    sender_part = product(weights[:, 64:], extended(feats, halo))
    fill_table(table, sender_part[:, :COARSE])
    tail[...] = sender_part[:, COARSE:]

    def body(step, carry):
        part = span(step, WIDTH)
        base = received[:, part]

        def edge(k, total):
            row = sources[pl.ds(k, 1), part]
            found = lane_gather(tail, COARSE // 128, row, read_table(table, COARSE // RADIX, row))
            silu, slopes = silu_and_slope(base + found)
            slope[k, :, part] = slopes
            return total + silu
        hidden[:, part] = lax.fori_loop(0, 8, edge, jnp.zeros((64, WIDTH), jnp.float32), unroll=4)
        return carry
    lax.fori_loop(0, 2048 // WIDTH, body, 0)
    aggregate = product(edge_out[...], hidden[...])
    pre = product(node_in[...], jnp.concatenate([feats, aggregate], axis=0)) + bias[:, 1:2]
    node_pre[...] = pre
    middle[...] = feats + product(node_out[...], pre * gate(pre))
    put_slabs(packed, spread_all(columns, middle[...], to_coarse[...]) * scale)
    pl.semaphore_wait(barrier, count)
    summing.run()
    for position in range(16):
        pooled[:, position * 128:position * 128 + 128] = summing.slab(position)


def coarse_kernel(factor, pooled, coarse_in, coarse_out, coarse_mix, biases, edges, to_fine, middle, cotangent,
                  up_in, up_out, output, grad_middle, grad_mixed, mixed_back, mixed_sum, up_grads, table, looked,
                  sums, columns, packed, mine, theirs, mine_back, theirs_back, swap_sems, *scratch):
    summing = WholeSum(16, packed, scratch)
    barrier = pltpu.get_barrier_semaphore()
    count = summing.greet(barrier)
    bias = bias_columns(biases)
    first = jnp.broadcast_to(summing.core == 0, (32, 2048))
    values = pooled[...]
    pre = product(coarse_in[...], values) + bias[:, 2:3]
    nodes = values + product(coarse_out[...], pre * gate(pre))
    mine[...] = mix_half(sums, table, columns, edges, 0, 1, jnp.where(first, nodes[:32], nodes[32:]))
    pl.semaphore_wait(barrier, count)
    swap = copy_to(mine, theirs, swap_sems.at[0], swap_sems.at[1], summing.sibling)
    swap.start()
    swap.wait()
    summed = jnp.concatenate([jnp.where(first, mine[...], theirs[...]), jnp.where(first, theirs[...], mine[...])],
                             axis=0)
    mixed_sum[...] = summed
    fill_table(table, nodes + product(coarse_mix[...], summed) * factor)
    read_all(looked, table, to_fine, WIDTH)
    both = jnp.concatenate([middle[...], looked[...]], axis=0)
    silu, slopes = silu_and_slope(product(up_in[...], both) + bias[:, 3:4])
    output[...] = middle[...] + product(up_out[...], silu)
    cot = cotangent[...]
    grad_pre = product_tn(up_out[...], cot) * slopes
    up_grads[0] = product_nt(grad_pre, both)
    up_grads[1] = jnp.concatenate(
        [product_nt(cot, silu), jnp.broadcast_to(jnp.sum(grad_pre, axis=1, keepdims=True), (64, 64))], axis=1)
    grad_both = product_tn(up_in[...], grad_pre)
    grad_middle[...] = cot + grad_both[:64]
    put_slabs(packed, spread_all(columns, grad_both[64:], to_fine[...]))
    summing.run(back=False)
    summing.back_core().start()
    own_half = jnp.concatenate([summing.half_out[position] for position in range(16)], axis=1)
    mine_back[...] = mix_half(sums, table, columns, edges, 1, 0, own_half)
    swap = copy_to(mine_back, theirs_back, swap_sems.at[2], swap_sems.at[3], summing.sibling)
    swap.start()
    summing.back_core().wait()
    for position in range(16):
        grad_mixed[:, position * 128:position * 128 + 128] = summing.slab(position)
    swap.wait()
    mixed_back[:32] = jnp.where(first, mine_back[...], theirs_back[...])
    mixed_back[32:] = jnp.where(first, theirs_back[...], mine_back[...])


def backward_kernel(factor, scale, grad_mixed, mixed_back, mixed_sum, pooled, coarse_in, coarse_out, coarse_mix,
                    biases, to_coarse, grad_middle, node_pre, hidden, slope, features, halo, sources, edge_in,
                    edge_out, node_in, node_out, up_grads, rows, grad_features, weight_sums, coarse_grads, table,
                    found, scratch, sums, columns, own, grad_halo, packed, arrived_ref, sent, arrived, *sum_refs):
    summing = WholeSum(8, packed, sum_refs)
    barrier = pltpu.get_barrier_semaphore()
    count = summing.greet(barrier)
    greet_sides(barrier)
    bias = bias_columns(biases)
    packed[4:6] = up_grads[...]
    packed[6:8] = jnp.zeros((2, 64, 128), jnp.float32)
    grad_mix_all = grad_mixed[...]
    coarse_grads[:, 256:384] = jnp.concatenate(
        [product_nt(grad_mix_all, mixed_sum[...]) * factor, jnp.zeros((64, 64), jnp.float32)], axis=1)
    grad_nodes = grad_mix_all + product_tn(coarse_mix[...], mixed_back[...]) * factor
    values = pooled[...]
    silu, slopes = silu_and_slope(product(coarse_in[...], values) + bias[:, 2:3])
    grad_pre = product_tn(coarse_out[...], grad_nodes) * slopes
    coarse_grads[:, 0:128] = jnp.concatenate([product_nt(grad_pre, values), product_nt(grad_nodes, silu)], axis=1)
    coarse_grads[:, 128:256] = jnp.broadcast_to(jnp.sum(grad_pre, axis=1, keepdims=True), (64, 128))
    fill_table(table, grad_nodes + product_tn(coarse_in[...], grad_pre))
    read_all(found, table, to_coarse, WIDTH)
    grad_mid = grad_middle[...] + found[...] * scale
    feats = features[...]
    silu, slopes = silu_and_slope(node_pre[...])
    aggregate = product(edge_out[...], hidden[...])
    grad_pre = product_tn(node_out[...], grad_mid) * slopes
    packed[0] = product_nt(grad_pre, jnp.concatenate([feats, aggregate], axis=0))
    node_bias = jnp.sum(grad_pre, axis=1, keepdims=True)
    grad_both = product_tn(node_in[...], grad_pre)
    grad_sum = grad_both[64:]
    packed[1] = jnp.concatenate(
        [product_nt(grad_mid, silu), product_nt(grad_sum, hidden[...])], axis=1)
    found[...] = grad_mid + grad_both[:64]
    scratch[...] = product_tn(edge_out[...], grad_sum)
    blocks = EXT // RADIX
    sums[...] = jnp.zeros(sums.shape, jnp.float32)
    fill_columns(columns, sources[...])

    def body(step, carry):
        part = span(step, WIDTH)
        base = scratch[:, part]

        def edge(k, total):
            grad_edge = base * slope[k, :, part]
            sums[...] += spread(grad_edge, blocks, sources[pl.ds(k, 1), part], columns[k, part])
            return total + grad_edge
        scratch[:, part] = lax.fori_loop(0, 8, edge, jnp.zeros((64, WIDTH), jnp.float32), unroll=4)
        return carry
    lax.fori_loop(0, 2048 // WIDTH, body, 0)
    grad_sent = gathered_sums(sums, blocks)
    grad_received = scratch[...]
    packed[2] = jnp.concatenate(
        [product_nt(grad_received, feats),
         product_nt(grad_sent, extended(feats, halo))], axis=1)
    packed[3] = jnp.concatenate(
        [jnp.broadcast_to(jnp.sum(grad_received, axis=1, keepdims=True), (64, 64)),
         jnp.broadcast_to(node_bias, (64, 64))], axis=1)
    weights = edge_in[...]
    back = product_tn(weights[:, 64:], grad_sent)
    own[...] = found[...] + product_tn(weights[:, :64], grad_received) + back[:, :2048]
    for slot in range(4):
        grad_halo[slot] = back[:, 2048 + slot * 128:2048 + slot * 128 + 128]
    pl.semaphore_wait(barrier, count + 4)
    for slot in range(4):
        side_copy(grad_halo, arrived_ref, sent, arrived, slot, True).start()

    def add_returned():
        columns, parts = [], []
        for slot in range(4):
            side_copy(grad_halo, arrived_ref, sent, arrived, slot, True).wait()
            there = jnp.broadcast_to(side_exists(True)[slot], (64, 128))
            parts.append(jnp.where(there, arrived_ref[slot], 0.0))
        indices = rows[...]
        lows = (jnp.concatenate([indices, indices], axis=0) & (RADIX - 1)).astype(jnp.float32).T
        index_row = jnp.concatenate([indices[slot:slot + 1, :] for slot in range(4)], axis=1)
        low_column = jnp.concatenate([lows[:, slot:slot + 1] for slot in range(4)], axis=0)
        blocks = COARSE // RADIX
        found = spread(jnp.concatenate(parts, axis=1), blocks, index_row, low_column)
        for block in range(blocks):
            part = slice(block * RADIX, (block + 1) * RADIX)
            grad_features[:, part] = own[:, part] + found[block * 64:block * 64 + 64]
    summing.run(add_returned)
    for position in range(8):
        weight_sums[position] = summing.slab(position)


def call(kernel, outs, scratch, *operands):
    return pl.pallas_call(
        kernel,
        out_shape=[jax.ShapeDtypeStruct(shape, jnp.float32) for shape in outs],
        in_specs=[pl.BlockSpec(memory_space=pltpu.VMEM)] * len(operands),
        out_specs=[pl.BlockSpec(memory_space=pltpu.VMEM)] * len(outs),
        scratch_shapes=[pltpu.VMEM(shape, dtype) for shape, dtype in scratch],
        compiler_params=pltpu.CompilerParams(vmem_limit_bytes=VMEM_LIMIT),
    )(*operands)


def copy_to(source, target, sent, arrived, device):
    return pltpu.make_async_remote_copy(
        src_ref=source, dst_ref=target, send_sem=sent, recv_sem=arrived, device_id=device, device_id_type=MESH)


def each(make, count):
    for k in range(1, count):
        make(k).start()
    for k in range(1, count):
        make(k).wait()


def turned(place, count):
    return jnp.where(place >= count, place - count, place)


def side_devices(back):
    gx, gy = lax.axis_index("gx"), lax.axis_index("gy")
    up, down = (lax.rem(gx + 1, 8), gy), (lax.rem(gx + 7, 8), gy)
    right, left = (gx, lax.rem(gy + 1, 32)), (gx, lax.rem(gy + 31, 32))
    return (down, up, left, right) if back else (up, down, right, left)


def side_exists(back):
    gx, gy = lax.axis_index("gx"), lax.axis_index("gy")
    below = (gx > 0, gx < 7, gy > 0, gy < 31)
    return (below[1], below[0], below[3], below[2]) if back else below


def greet_sides(barrier):
    for device in side_devices(False):
        pl.semaphore_signal(barrier, inc=1, device_id=device, device_id_type=MESH)


class WholeSum:
    def __init__(self, slabs, x_ref, scratch):
        (self.half, self.core_parts, self.flat_parts, self.piece, self.line_parts, self.half_out, self.other,
         self.core_sems, self.flat_sent, self.flat_arrived, self.line_sent, self.line_arrived,
         self.back_sent, self.back_arrived) = scratch
        self.slabs, self.rows, self.x_ref = slabs, 2 * slabs, x_ref
        gx, gy = lax.axis_index("gx"), lax.axis_index("gy")
        self.x, self.y = gx // 2, gy // 8
        self.core, self.z = gx - 2 * self.x, gy - 8 * self.y
        self.gx, self.gy = gx, gy
        self.sibling = (gx + 1 - 2 * self.core, gy)
        self.xs = [turned(self.x + k, 4) for k in range(4)]
        self.ys = [turned(self.y + k, 4) for k in range(4)]
        self.zs = [turned(self.z + k, 8) for k in range(8)]

    def flat_device(self, k):
        return (self.xs[k // 4] * 2 + self.core, self.ys[k % 4] * 8 + self.z)

    def line_device(self, k):
        return (self.gx, self.y * 8 + self.zs[k])

    def chunk(self, ref, k):
        x, y = self.xs[k // 4], self.ys[k % 4]
        if self.rows == 32:
            return ref.at[x * 4 + y]
        high = y // 2
        return ref.at[x * 2 + high, pl.ds(pl.multiple_of((y - 2 * high) * 16, 16), 16)]

    def own_rows(self, core):
        return pl.ds(pl.multiple_of(core * 32, 32), 32)

    def greet(self, barrier):
        devices = ([self.sibling] + [self.line_device(k) for k in range(1, 8)]
                   + [self.flat_device(k) for k in range(1, 16)])
        for device in devices:
            pl.semaphore_signal(barrier, inc=1, device_id=device, device_id_type=MESH)
        return len(devices)

    def to_core(self):
        return copy_to(self.x_ref.at[:, self.own_rows(1 - self.core)], self.core_parts,
                       self.core_sems.at[0], self.core_sems.at[1], self.sibling)

    def to_flat(self, k):
        return copy_to(self.chunk(self.half, k), self.flat_parts.at[k], self.flat_sent.at[k],
                       self.flat_arrived.at[k], self.flat_device(k))

    def to_line(self, k):
        return copy_to(self.piece, self.line_parts.at[self.z], self.line_sent.at[k], self.line_arrived.at[k],
                       self.line_device(k))

    def back_flat(self, k):
        mine = self.chunk(self.half_out, 0)
        return copy_to(mine, mine, self.back_sent.at[k], self.back_arrived.at[k], self.flat_device(k))

    def back_core(self):
        return copy_to(self.half_out, self.other, self.core_sems.at[2], self.core_sems.at[3], self.sibling)

    def run(self, beside=None, back=True):
        self.to_core().start()
        if beside is not None:
            beside()
        self.to_core().wait()
        self.half[...] = self.x_ref[:, self.own_rows(self.core)] + self.core_parts[...]
        each(self.to_flat, 16)
        total = self.chunk(self.half, 0)[...]
        for k in range(1, 16):
            total = total + self.flat_parts[k]
        self.piece[...] = total
        self.line_parts[self.z] = total
        each(self.to_line, 8)
        total = self.line_parts[0]
        for k in range(1, 8):
            total = total + self.line_parts[k]
        self.chunk(self.half_out, 0)[...] = total
        each(self.back_flat, 16)
        if back:
            self.back_core().start()
            self.back_core().wait()

    def slab(self, position):
        first = jnp.broadcast_to(self.core == 0, (32, 128))
        own, other = self.half_out[position], self.other[position]
        return jnp.concatenate([jnp.where(first, own, other), jnp.where(first, other, own)], axis=0)


def sum_scratch(slabs):
    rows, dma = 2 * slabs, pltpu.SemaphoreType.DMA
    half = pltpu.VMEM((slabs, 32, 128), jnp.float32)
    return [half, half, pltpu.VMEM((16, rows, 128), jnp.float32), pltpu.VMEM((rows, 128), jnp.float32),
            pltpu.VMEM((8, rows, 128), jnp.float32), half, half,
            dma((4,)), dma((16,)), dma((16,)), dma((8,)), dma((8,)), dma((16,)), dma((16,))]


def remote_call(kernel, outs, scratch, collective_id, *operands):
    return pl.pallas_call(
        kernel,
        out_shape=[jax.ShapeDtypeStruct(shape, jnp.float32) for shape in outs],
        in_specs=[pl.BlockSpec(memory_space=pltpu.VMEM)] * len(operands),
        out_specs=[pl.BlockSpec(memory_space=pltpu.VMEM)] * len(outs),
        scratch_shapes=scratch,
        compiler_params=pltpu.CompilerParams(collective_id=collective_id, has_side_effects=True,
                                             vmem_limit_bytes=VMEM_LIMIT),
    )(*operands)


def side_copy(packets, arrived_ref, sent, arrived, slot, back):
    return copy_to(packets.at[slot], arrived_ref.at[slot], sent.at[slot], arrived.at[slot], side_devices(back)[slot])


def halo_kernel(features, rows, halo, table, packets, arrived_ref, sent, arrived):
    barrier = pltpu.get_barrier_semaphore()
    greet_sides(barrier)
    fill_table(table, features[...])
    for slot in range(4):
        packets[slot] = read_table(table, COARSE // RADIX, rows[slot:slot + 1, :])
    pl.semaphore_wait(barrier, 4)
    for slot in range(4):
        side_copy(packets, arrived_ref, sent, arrived, slot, False).start()
    for slot in range(4):
        side_copy(packets, arrived_ref, sent, arrived, slot, False).wait()
        there = jnp.broadcast_to(side_exists(False)[slot], (64, 128))
        halo[slot] = jnp.where(there, arrived_ref[slot], 0.0)


def exchange(features, rows):
    dma = pltpu.SemaphoreType.DMA
    slots = pltpu.VMEM((4, 64, 128), jnp.float32)
    halo, = remote_call(
        halo_kernel, [(4, 64, 128)],
        [pltpu.VMEM((COARSE // RADIX * 64, 2 * RADIX), jnp.bfloat16), slots, slots, dma((4,)), dma((4,))],
        1, features, rows)
    return halo


def unpack_kernel(output, grad_features, weight_sums, coarse_grads, out, out_features, grad_edge_in, grad_edge_out,
                  grad_node_in, grad_node_out, grad_coarse_in, grad_coarse_out, grad_coarse_mix, grad_up_in,
                  grad_up_out, grad_biases):
    out[...] = output[...]
    out_features[...] = grad_features[...]
    grad_node_in[...] = weight_sums[0]
    pair = weight_sums[1]
    grad_node_out[...] = pair[:, :64]
    grad_edge_out[...] = pair[:, 64:]
    grad_edge_in[...] = weight_sums[2]
    grad_up_in[...] = weight_sums[4]
    last = weight_sums[5]
    grad_up_out[...] = last[:, :64]
    grad_coarse_in[...] = coarse_grads[:, 0:64]
    grad_coarse_out[...] = coarse_grads[:, 64:128]
    grad_coarse_mix[...] = coarse_grads[:, 256:320]
    fine_bias, up_bias, coarse_bias = weight_sums[3].T, last.T, coarse_grads[:, 128:256].T
    grad_biases[...] = jnp.concatenate(
        [fine_bias[0:1], fine_bias[64:65], coarse_bias[0:1], up_bias[64:65]], axis=0)


def local(
    features,
    cotangent,
    edge_src,
    send_rows,
    fine_to_coarse,
    coarse_to_fine,
    coarse_edges,
    edge_in,
    edge_out,
    node_in,
    node_out,
    coarse_in,
    coarse_out,
    coarse_mix,
    up_in,
    up_out,
    biases,
):
    scale = (COARSE / (features.shape[1] * lax.axis_size("gx") * lax.axis_size("gy"))) ** 0.5
    factor = (COARSE / coarse_edges.shape[1]) ** 0.5
    f32, dma = jnp.float32, pltpu.SemaphoreType.DMA
    to_coarse, to_fine = fine_to_coarse.reshape(1, -1), coarse_to_fine.reshape(1, -1)
    table = pltpu.VMEM((EXT // RADIX * 64, 2 * RADIX), jnp.bfloat16)
    sums, columns = pltpu.VMEM((EXT // RADIX * 64, RADIX), f32), pltpu.VMEM((8, 2048, 1), f32)
    wide, half = pltpu.VMEM((64, 2048), f32), pltpu.VMEM((32, 2048), f32)
    slots = pltpu.VMEM((4, 64, 128), f32)
    halo = exchange(features, send_rows)
    middle, slope, hidden, node_pre, pooled = remote_call(
        partial(fine_forward_kernel, scale),
        [(64, 2048), (8, 64, 2048), (64, 2048), (64, 2048), (64, 2048)],
        [table, wide, columns, pltpu.VMEM((16, 64, 128), f32), pltpu.VMEM((64, 512), f32), *sum_scratch(16)], 2,
        features, halo, edge_src, to_coarse, edge_in, edge_out, node_in, node_out, biases)
    output, grad_middle, grad_mixed, mixed_back, mixed_sum, up_grads = remote_call(
        partial(coarse_kernel, factor),
        [(64, 2048), (64, 2048), (64, 2048), (64, 2048), (64, 2048), (2, 64, 128)],
        [table, wide, sums, columns, pltpu.VMEM((16, 64, 128), f32), half, half, half, half, dma((4,)),
         *sum_scratch(16)], 3,
        pooled, coarse_in, coarse_out, coarse_mix, biases, coarse_edges, to_fine, middle, cotangent, up_in, up_out)
    grad_features, weight_sums, coarse_grads = remote_call(
        partial(backward_kernel, factor, scale),
        [(64, 2048), (8, 64, 128), (64, 384)],
        [table, wide, wide, sums, columns, wide, slots, pltpu.VMEM((8, 64, 128), f32), slots, dma((4,)), dma((4,)),
         *sum_scratch(8)], 4,
        grad_mixed, mixed_back, mixed_sum, pooled, coarse_in, coarse_out, coarse_mix, biases, to_coarse,
        grad_middle, node_pre, hidden, slope, features, halo, edge_src, edge_in, edge_out, node_in, node_out,
        up_grads, send_rows)
    (out, out_features, grad_edge_in, grad_edge_out, grad_node_in, grad_node_out, grad_coarse_in, grad_coarse_out,
     grad_coarse_mix, grad_up_in, grad_up_out, grad_biases) = call(
        unpack_kernel,
        [(64, 2048), (64, 2048), (64, 128), (64, 64), (64, 128), (64, 64), (64, 64), (64, 64), (64, 64), (64, 128),
         (64, 64), (4, 64)], [], output, grad_features, weight_sums, coarse_grads)
    return (out, out_features, grad_edge_in, grad_edge_out, grad_node_in, grad_node_out, grad_coarse_in,
            grad_coarse_out, grad_coarse_mix, grad_up_in, grad_up_out, grad_biases)


def solution(mesh):
    in_specs = (
        P(None, ("gx", "gy")),
        P(None, ("gx", "gy")),
        P(None, ("gx", "gy")),
        P(None, ("gx", "gy")),
        P(("gx", "gy")),
        P(("gx", "gy")),
        P(),
        P(),
        P(),
        P(),
        P(),
        P(),
        P(),
        P(),
        P(),
        P(),
        P(),
    )
    out_specs = (
        P(None, ("gx", "gy")),
        P(None, ("gx", "gy")),
        P(),
        P(),
        P(),
        P(),
        P(),
        P(),
        P(),
        P(),
        P(),
        P(),
    )
    return jax.shard_map(local, mesh=mesh, in_specs=in_specs, out_specs=out_specs, check_vma=False)
```

```python
from functools import partial

import jax
import jax.numpy as jnp
from jax import lax
from jax.experimental import pallas as pl
from jax.experimental.pallas import tpu as pltpu
from jax.sharding import PartitionSpec as P

COARSE = 2048
EXT = 2560
RADIX = 256
SHIFT = 8
WIDTH = 2048
VMEM_LIMIT = 44 * 2**20


MESH = pl.DeviceIdType.MESH


def halves(values):
    high = values.astype(jnp.bfloat16)
    return high, (values - high.astype(jnp.float32)).astype(jnp.bfloat16)


def product(left, right):
    left_high, left_low = halves(left)
    right_high, right_low = halves(right)
    return jnp.dot(jnp.concatenate([left_high, left_low, left_high], axis=1),
                   jnp.concatenate([right_high, right_high, right_low], axis=0),
                   preferred_element_type=jnp.float32)


def product_nt(left, right):
    left_high, left_low = halves(left)
    right_high, right_low = halves(right)
    return lax.dot_general(jnp.concatenate([left_high, left_low, left_high], axis=1),
                           jnp.concatenate([right_high, right_high, right_low], axis=1),
                           (((1,), (1,)), ((), ())), preferred_element_type=jnp.float32)


def product_tn(left, right):
    return product(left.T, right)


def selector(index_row):
    rows = lax.broadcasted_iota(jnp.int32, (RADIX, index_row.shape[1]), 0).astype(jnp.bfloat16)
    low = (index_row & (RADIX - 1)).astype(jnp.float32).astype(jnp.bfloat16)
    return jnp.where(rows == low, jnp.bfloat16(1), jnp.bfloat16(0))


def fill_table(table_ref, values):
    high, low = halves(values)
    for block in range(values.shape[1] // RADIX):
        columns = slice(block * RADIX, (block + 1) * RADIX)
        rows = slice(block * values.shape[0], (block + 1) * values.shape[0])
        table_ref[rows, :RADIX] = high[:, columns]
        table_ref[rows, RADIX:] = low[:, columns]


def read_table(table_ref, blocks, index_row, height=64):
    picked = selector(index_row)
    found = jnp.dot(table_ref[:blocks * height], jnp.concatenate([picked, picked], axis=0),
                    preferred_element_type=jnp.float32)
    chosen = jnp.broadcast_to(index_row >> SHIFT, (height, index_row.shape[1]))
    total = found[:height]
    for block in range(1, blocks):
        total = jnp.where(chosen == block, found[block * height:(block + 1) * height], total)
    return total


def lane_gather(table_ref, first, index_row, start):
    pieces = []
    for piece in range(index_row.shape[1] // 128):
        row = index_row[:, piece * 128:piece * 128 + 128]
        lanes = jnp.broadcast_to(row & 127, (64, 128))
        chosen = jnp.broadcast_to(row >> 7, (64, 128))
        total = start[:, piece * 128:piece * 128 + 128]
        for block in range(table_ref.shape[1] // 128):
            found = jnp.take_along_axis(table_ref[:, block * 128:block * 128 + 128], lanes, axis=1)
            total = jnp.where(chosen == first + block, found, total)
        pieces.append(total)
    return jnp.concatenate(pieces, axis=1)


def spread(values, blocks, index_row, low_column):
    high, low = halves(values)
    chosen = jnp.broadcast_to(index_row >> SHIFT, (values.shape[0], index_row.shape[1]))
    parts = []
    for block in range(blocks):
        mask = jnp.where(chosen == block, 1.0, 0.0).astype(jnp.bfloat16)
        parts.append(jnp.concatenate([high * mask, low * mask], axis=1))
    lanes = lax.broadcasted_iota(jnp.int32, (low_column.shape[0], RADIX), 1).astype(jnp.bfloat16)
    picked = jnp.where(lanes == low_column.astype(jnp.bfloat16), jnp.bfloat16(1), jnp.bfloat16(0))
    return jnp.dot(jnp.concatenate(parts, axis=0), jnp.concatenate([picked, picked], axis=0),
                   preferred_element_type=jnp.float32)


def fill_columns(columns, rows):
    count = rows.shape[0]
    if count < 8:
        rows = jnp.concatenate([rows] * (8 // count), axis=0)
    turned = (rows & (RADIX - 1)).astype(jnp.float32).T
    for step in range(count):
        columns[step] = turned[:, step:step + 1]


def gathered_sums(sums_ref, blocks, height=64):
    return jnp.concatenate(
        [sums_ref[block * height:(block + 1) * height] for block in range(blocks)], axis=1)


def span(position, size):
    return pl.ds(pl.multiple_of(position * size, size), size)


def read_all(out_ref, table_ref, index_ref, width):
    def body(step, carry):
        part = span(step, width)
        out_ref[:, part] = read_table(table_ref, COARSE // RADIX, index_ref[:, part])
        return carry
    lax.fori_loop(0, index_ref.shape[1] // width, body, 0)


def spread_all(columns, values, index_row):
    blocks = COARSE // RADIX
    fill_columns(columns, index_row)
    found = spread(values, blocks, index_row, columns[0])
    return jnp.concatenate([found[block * 64:block * 64 + 64] for block in range(blocks)], axis=1)


def mix_half(sums_ref, table_ref, columns, edges_ref, sender, receiver, values):
    blocks = COARSE // RADIX
    used = blocks * 32
    fill_table(table_ref, values)
    sums_ref[:used] = jnp.zeros((used, RADIX), jnp.float32)
    fill_columns(columns, jnp.concatenate(
        [edges_ref[receiver:receiver + 1, step * 2048:step * 2048 + 2048] for step in range(4)], axis=0))

    def body(step, carry):
        part = span(step, 2048)
        found = read_table(table_ref, blocks, edges_ref[sender:sender + 1, part], 32)
        sums_ref[:used] += spread(found, blocks, edges_ref[receiver:receiver + 1, part], columns[step])
        return carry
    lax.fori_loop(0, 4, body, 0, unroll=4)
    return gathered_sums(sums_ref, blocks, 32)


def bias_columns(biases):
    rows = biases[...]
    return jnp.concatenate([rows, rows], axis=0).T


def extended(features, halo):
    return jnp.concatenate([features] + [halo[slot] for slot in range(4)], axis=1)


def put_slabs(out, values):
    for position in range(16):
        out[position] = values[:, position * 128:position * 128 + 128]


def gate(values):
    return 1.0 / (1.0 + jnp.exp(-values))


def silu_and_slope(values):
    opened = gate(values)
    silu = values * opened
    return silu, opened + silu * (1.0 - opened)


def fine_forward_kernel(scale, features, halo, sources, to_coarse, edge_in, edge_out, node_in, node_out, biases,
                        middle, slope, hidden, node_pre, pooled, table, received, columns, packed, tail, *scratch):
    summing = WholeSum(16, packed, scratch)
    barrier = pltpu.get_barrier_semaphore()
    count = summing.greet(barrier)
    bias = bias_columns(biases)
    feats = features[...]
    weights = edge_in[...]
    received[...] = product(weights[:, :64], feats) + bias[:, 0:1]
    sender_part = product(weights[:, 64:], extended(feats, halo))
    fill_table(table, sender_part[:, :COARSE])
    tail[...] = sender_part[:, COARSE:]

    def body(step, carry):
        part = span(step, WIDTH)
        base = received[:, part]

        def edge(k, total):
            row = sources[pl.ds(k, 1), part]
            found = lane_gather(tail, COARSE // 128, row, read_table(table, COARSE // RADIX, row))
            silu, slopes = silu_and_slope(base + found)
            slope[k, :, part] = slopes
            return total + silu
        hidden[:, part] = lax.fori_loop(0, 8, edge, jnp.zeros((64, WIDTH), jnp.float32), unroll=4)
        return carry
    lax.fori_loop(0, 2048 // WIDTH, body, 0)
    aggregate = product(edge_out[...], hidden[...])
    pre = product(node_in[...], jnp.concatenate([feats, aggregate], axis=0)) + bias[:, 1:2]
    node_pre[...] = pre
    middle[...] = feats + product(node_out[...], pre * gate(pre))
    put_slabs(packed, spread_all(columns, middle[...], to_coarse[...]) * scale)
    pl.semaphore_wait(barrier, count)
    summing.run()
    for position in range(16):
        pooled[:, position * 128:position * 128 + 128] = summing.slab(position)


def coarse_kernel(factor, pooled, coarse_in, coarse_out, coarse_mix, biases, edges, to_fine, middle, cotangent,
                  up_in, up_out, output, grad_middle, grad_mixed, mixed_back, mixed_sum, up_grads, table, looked,
                  sums, columns, packed, mine, theirs, mine_back, theirs_back, swap_sems, *scratch):
    summing = WholeSum(16, packed, scratch)
    barrier = pltpu.get_barrier_semaphore()
    count = summing.greet(barrier)
    bias = bias_columns(biases)
    first = jnp.broadcast_to(summing.core == 0, (32, 2048))
    values = pooled[...]
    pre = product(coarse_in[...], values) + bias[:, 2:3]
    nodes = values + product(coarse_out[...], pre * gate(pre))
    mine[...] = mix_half(sums, table, columns, edges, 0, 1, jnp.where(first, nodes[:32], nodes[32:]))
    pl.semaphore_wait(barrier, count)
    swap = copy_to(mine, theirs, swap_sems.at[0], swap_sems.at[1], summing.sibling)
    swap.start()
    swap.wait()
    summed = jnp.concatenate([jnp.where(first, mine[...], theirs[...]), jnp.where(first, theirs[...], mine[...])],
                             axis=0)
    mixed_sum[...] = summed
    fill_table(table, nodes + product(coarse_mix[...], summed) * factor)
    read_all(looked, table, to_fine, WIDTH)
    both = jnp.concatenate([middle[...], looked[...]], axis=0)
    silu, slopes = silu_and_slope(product(up_in[...], both) + bias[:, 3:4])
    output[...] = middle[...] + product(up_out[...], silu)
    cot = cotangent[...]
    grad_pre = product_tn(up_out[...], cot) * slopes
    up_grads[0] = product_nt(grad_pre, both)
    up_grads[1] = jnp.concatenate(
        [product_nt(cot, silu), jnp.broadcast_to(jnp.sum(grad_pre, axis=1, keepdims=True), (64, 64))], axis=1)
    grad_both = product_tn(up_in[...], grad_pre)
    grad_middle[...] = cot + grad_both[:64]
    put_slabs(packed, spread_all(columns, grad_both[64:], to_fine[...]))
    summing.run(back=False)
    summing.back_core().start()
    own_half = jnp.concatenate([summing.half_out[position] for position in range(16)], axis=1)
    mine_back[...] = mix_half(sums, table, columns, edges, 1, 0, own_half)
    swap = copy_to(mine_back, theirs_back, swap_sems.at[2], swap_sems.at[3], summing.sibling)
    swap.start()
    summing.back_core().wait()
    for position in range(16):
        grad_mixed[:, position * 128:position * 128 + 128] = summing.slab(position)
    swap.wait()
    mixed_back[:32] = jnp.where(first, mine_back[...], theirs_back[...])
    mixed_back[32:] = jnp.where(first, theirs_back[...], mine_back[...])


def backward_kernel(factor, scale, grad_mixed, mixed_back, mixed_sum, pooled, coarse_in, coarse_out, coarse_mix,
                    biases, to_coarse, grad_middle, node_pre, hidden, slope, features, halo, sources, edge_in,
                    edge_out, node_in, node_out, up_grads, rows, grad_features, weight_sums, coarse_grads, table,
                    found, scratch, sums, columns, own, grad_halo, packed, arrived_ref, sent, arrived, *sum_refs):
    summing = WholeSum(8, packed, sum_refs)
    barrier = pltpu.get_barrier_semaphore()
    count = summing.greet(barrier)
    greet_sides(barrier)
    bias = bias_columns(biases)
    packed[4:6] = up_grads[...]
    packed[6:8] = jnp.zeros((2, 64, 128), jnp.float32)
    grad_mix_all = grad_mixed[...]
    coarse_grads[:, 256:384] = jnp.concatenate(
        [product_nt(grad_mix_all, mixed_sum[...]) * factor, jnp.zeros((64, 64), jnp.float32)], axis=1)
    grad_nodes = grad_mix_all + product_tn(coarse_mix[...], mixed_back[...]) * factor
    values = pooled[...]
    silu, slopes = silu_and_slope(product(coarse_in[...], values) + bias[:, 2:3])
    grad_pre = product_tn(coarse_out[...], grad_nodes) * slopes
    coarse_grads[:, 0:128] = jnp.concatenate([product_nt(grad_pre, values), product_nt(grad_nodes, silu)], axis=1)
    coarse_grads[:, 128:256] = jnp.broadcast_to(jnp.sum(grad_pre, axis=1, keepdims=True), (64, 128))
    fill_table(table, grad_nodes + product_tn(coarse_in[...], grad_pre))
    read_all(found, table, to_coarse, WIDTH)
    grad_mid = grad_middle[...] + found[...] * scale
    feats = features[...]
    silu, slopes = silu_and_slope(node_pre[...])
    aggregate = product(edge_out[...], hidden[...])
    grad_pre = product_tn(node_out[...], grad_mid) * slopes
    packed[0] = product_nt(grad_pre, jnp.concatenate([feats, aggregate], axis=0))
    node_bias = jnp.sum(grad_pre, axis=1, keepdims=True)
    grad_both = product_tn(node_in[...], grad_pre)
    grad_sum = grad_both[64:]
    packed[1] = jnp.concatenate(
        [product_nt(grad_mid, silu), product_nt(grad_sum, hidden[...])], axis=1)
    found[...] = grad_mid + grad_both[:64]
    scratch[...] = product_tn(edge_out[...], grad_sum)
    blocks = EXT // RADIX
    sums[...] = jnp.zeros(sums.shape, jnp.float32)
    fill_columns(columns, sources[...])

    def body(step, carry):
        part = span(step, WIDTH)
        base = scratch[:, part]

        def edge(k, total):
            grad_edge = base * slope[k, :, part]
            sums[...] += spread(grad_edge, blocks, sources[pl.ds(k, 1), part], columns[k, part])
            return total + grad_edge
        scratch[:, part] = lax.fori_loop(0, 8, edge, jnp.zeros((64, WIDTH), jnp.float32), unroll=4)
        return carry
    lax.fori_loop(0, 2048 // WIDTH, body, 0)
    grad_sent = gathered_sums(sums, blocks)
    grad_received = scratch[...]
    packed[2] = jnp.concatenate(
        [product_nt(grad_received, feats),
         product_nt(grad_sent, extended(feats, halo))], axis=1)
    packed[3] = jnp.concatenate(
        [jnp.broadcast_to(jnp.sum(grad_received, axis=1, keepdims=True), (64, 64)),
         jnp.broadcast_to(node_bias, (64, 64))], axis=1)
    weights = edge_in[...]
    back = product_tn(weights[:, 64:], grad_sent)
    own[...] = found[...] + product_tn(weights[:, :64], grad_received) + back[:, :2048]
    for slot in range(4):
        grad_halo[slot] = back[:, 2048 + slot * 128:2048 + slot * 128 + 128]
    pl.semaphore_wait(barrier, count + 4)
    for slot in range(4):
        side_copy(grad_halo, arrived_ref, sent, arrived, slot, True).start()

    def add_returned():
        columns, parts = [], []
        for slot in range(4):
            side_copy(grad_halo, arrived_ref, sent, arrived, slot, True).wait()
            there = jnp.broadcast_to(side_exists(True)[slot], (64, 128))
            parts.append(jnp.where(there, arrived_ref[slot], 0.0))
        indices = rows[...]
        lows = (jnp.concatenate([indices, indices], axis=0) & (RADIX - 1)).astype(jnp.float32).T
        index_row = jnp.concatenate([indices[slot:slot + 1, :] for slot in range(4)], axis=1)
        low_column = jnp.concatenate([lows[:, slot:slot + 1] for slot in range(4)], axis=0)
        blocks = COARSE // RADIX
        found = spread(jnp.concatenate(parts, axis=1), blocks, index_row, low_column)
        for block in range(blocks):
            part = slice(block * RADIX, (block + 1) * RADIX)
            grad_features[:, part] = own[:, part] + found[block * 64:block * 64 + 64]
    summing.run(add_returned)
    for position in range(8):
        weight_sums[position] = summing.slab(position)


def call(kernel, outs, scratch, *operands):
    return pl.pallas_call(
        kernel,
        out_shape=[jax.ShapeDtypeStruct(shape, jnp.float32) for shape in outs],
        in_specs=[pl.BlockSpec(memory_space=pltpu.VMEM)] * len(operands),
        out_specs=[pl.BlockSpec(memory_space=pltpu.VMEM)] * len(outs),
        scratch_shapes=[pltpu.VMEM(shape, dtype) for shape, dtype in scratch],
        compiler_params=pltpu.CompilerParams(vmem_limit_bytes=VMEM_LIMIT),
    )(*operands)


def copy_to(source, target, sent, arrived, device):
    return pltpu.make_async_remote_copy(
        src_ref=source, dst_ref=target, send_sem=sent, recv_sem=arrived, device_id=device, device_id_type=MESH)


def each(make, count):
    for k in range(1, count):
        make(k).start()
    for k in range(1, count):
        make(k).wait()


def turned(place, count):
    return jnp.where(place >= count, place - count, place)


def side_devices(back):
    gx, gy = lax.axis_index("gx"), lax.axis_index("gy")
    up, down = (lax.rem(gx + 1, 8), gy), (lax.rem(gx + 7, 8), gy)
    right, left = (gx, lax.rem(gy + 1, 32)), (gx, lax.rem(gy + 31, 32))
    return (down, up, left, right) if back else (up, down, right, left)


def side_exists(back):
    gx, gy = lax.axis_index("gx"), lax.axis_index("gy")
    below = (gx > 0, gx < 7, gy > 0, gy < 31)
    return (below[1], below[0], below[3], below[2]) if back else below


def greet_sides(barrier):
    for device in side_devices(False):
        pl.semaphore_signal(barrier, inc=1, device_id=device, device_id_type=MESH)


class WholeSum:
    def __init__(self, slabs, x_ref, scratch):
        (self.half, self.core_parts, self.flat_parts, self.piece, self.line_parts, self.half_out, self.other,
         self.core_sems, self.flat_sent, self.flat_arrived, self.line_sent, self.line_arrived,
         self.back_sent, self.back_arrived) = scratch
        self.slabs, self.rows, self.x_ref = slabs, 2 * slabs, x_ref
        gx, gy = lax.axis_index("gx"), lax.axis_index("gy")
        self.x, self.y = gx // 2, gy // 8
        self.core, self.z = gx - 2 * self.x, gy - 8 * self.y
        self.gx, self.gy = gx, gy
        self.sibling = (gx + 1 - 2 * self.core, gy)
        self.xs = [turned(self.x + k, 4) for k in range(4)]
        self.ys = [turned(self.y + k, 4) for k in range(4)]
        self.zs = [turned(self.z + k, 8) for k in range(8)]

    def flat_device(self, k):
        return (self.xs[k // 4] * 2 + self.core, self.ys[k % 4] * 8 + self.z)

    def line_device(self, k):
        return (self.gx, self.y * 8 + self.zs[k])

    def chunk(self, ref, k):
        x, y = self.xs[k // 4], self.ys[k % 4]
        if self.rows == 32:
            return ref.at[x * 4 + y]
        high = y // 2
        return ref.at[x * 2 + high, pl.ds(pl.multiple_of((y - 2 * high) * 16, 16), 16)]

    def own_rows(self, core):
        return pl.ds(pl.multiple_of(core * 32, 32), 32)

    def greet(self, barrier):
        devices = ([self.sibling] + [self.line_device(k) for k in range(1, 8)]
                   + [self.flat_device(k) for k in range(1, 16)])
        for device in devices:
            pl.semaphore_signal(barrier, inc=1, device_id=device, device_id_type=MESH)
        return len(devices)

    def to_core(self):
        return copy_to(self.x_ref.at[:, self.own_rows(1 - self.core)], self.core_parts,
                       self.core_sems.at[0], self.core_sems.at[1], self.sibling)

    def to_flat(self, k):
        return copy_to(self.chunk(self.half, k), self.flat_parts.at[k], self.flat_sent.at[k],
                       self.flat_arrived.at[k], self.flat_device(k))

    def to_line(self, k):
        return copy_to(self.piece, self.line_parts.at[self.z], self.line_sent.at[k], self.line_arrived.at[k],
                       self.line_device(k))

    def back_flat(self, k):
        mine = self.chunk(self.half_out, 0)
        return copy_to(mine, mine, self.back_sent.at[k], self.back_arrived.at[k], self.flat_device(k))

    def back_core(self):
        return copy_to(self.half_out, self.other, self.core_sems.at[2], self.core_sems.at[3], self.sibling)

    def run(self, beside=None, back=True):
        self.to_core().start()
        if beside is not None:
            beside()
        self.to_core().wait()
        self.half[...] = self.x_ref[:, self.own_rows(self.core)] + self.core_parts[...]
        each(self.to_flat, 16)
        total = self.chunk(self.half, 0)[...]
        for k in range(1, 16):
            total = total + self.flat_parts[k]
        self.piece[...] = total
        self.line_parts[self.z] = total
        each(self.to_line, 8)
        total = self.line_parts[0]
        for k in range(1, 8):
            total = total + self.line_parts[k]
        self.chunk(self.half_out, 0)[...] = total
        each(self.back_flat, 16)
        if back:
            self.back_core().start()
            self.back_core().wait()

    def slab(self, position):
        first = jnp.broadcast_to(self.core == 0, (32, 128))
        own, other = self.half_out[position], self.other[position]
        return jnp.concatenate([jnp.where(first, own, other), jnp.where(first, other, own)], axis=0)


def sum_scratch(slabs):
    rows, dma = 2 * slabs, pltpu.SemaphoreType.DMA
    half = pltpu.VMEM((slabs, 32, 128), jnp.float32)
    return [half, half, pltpu.VMEM((16, rows, 128), jnp.float32), pltpu.VMEM((rows, 128), jnp.float32),
            pltpu.VMEM((8, rows, 128), jnp.float32), half, half,
            dma((4,)), dma((16,)), dma((16,)), dma((8,)), dma((8,)), dma((16,)), dma((16,))]


def remote_call(kernel, outs, scratch, collective_id, *operands):
    return pl.pallas_call(
        kernel,
        out_shape=[jax.ShapeDtypeStruct(shape, jnp.float32) for shape in outs],
        in_specs=[pl.BlockSpec(memory_space=pltpu.VMEM)] * len(operands),
        out_specs=[pl.BlockSpec(memory_space=pltpu.VMEM)] * len(outs),
        scratch_shapes=scratch,
        compiler_params=pltpu.CompilerParams(collective_id=collective_id, has_side_effects=True,
                                             vmem_limit_bytes=VMEM_LIMIT),
    )(*operands)


def side_copy(packets, arrived_ref, sent, arrived, slot, back):
    return copy_to(packets.at[slot], arrived_ref.at[slot], sent.at[slot], arrived.at[slot], side_devices(back)[slot])


def halo_kernel(features, rows, halo, table, packets, arrived_ref, sent, arrived):
    barrier = pltpu.get_barrier_semaphore()
    greet_sides(barrier)
    fill_table(table, features[...])
    for slot in range(4):
        packets[slot] = read_table(table, COARSE // RADIX, rows[slot:slot + 1, :])
    pl.semaphore_wait(barrier, 4)
    for slot in range(4):
        side_copy(packets, arrived_ref, sent, arrived, slot, False).start()
    for slot in range(4):
        side_copy(packets, arrived_ref, sent, arrived, slot, False).wait()
        there = jnp.broadcast_to(side_exists(False)[slot], (64, 128))
        halo[slot] = jnp.where(there, arrived_ref[slot], 0.0)


def exchange(features, rows):
    dma = pltpu.SemaphoreType.DMA
    slots = pltpu.VMEM((4, 64, 128), jnp.float32)
    halo, = remote_call(
        halo_kernel, [(4, 64, 128)],
        [pltpu.VMEM((COARSE // RADIX * 64, 2 * RADIX), jnp.bfloat16), slots, slots, dma((4,)), dma((4,))],
        1, features, rows)
    return halo


def unpack_kernel(output, grad_features, weight_sums, coarse_grads, out, out_features, grad_edge_in, grad_edge_out,
                  grad_node_in, grad_node_out, grad_coarse_in, grad_coarse_out, grad_coarse_mix, grad_up_in,
                  grad_up_out, grad_biases):
    out[...] = output[...]
    out_features[...] = grad_features[...]
    grad_node_in[...] = weight_sums[0]
    pair = weight_sums[1]
    grad_node_out[...] = pair[:, :64]
    grad_edge_out[...] = pair[:, 64:]
    grad_edge_in[...] = weight_sums[2]
    grad_up_in[...] = weight_sums[4]
    last = weight_sums[5]
    grad_up_out[...] = last[:, :64]
    grad_coarse_in[...] = coarse_grads[:, 0:64]
    grad_coarse_out[...] = coarse_grads[:, 64:128]
    grad_coarse_mix[...] = coarse_grads[:, 256:320]
    fine_bias, up_bias, coarse_bias = weight_sums[3].T, last.T, coarse_grads[:, 128:256].T
    grad_biases[...] = jnp.concatenate(
        [fine_bias[0:1], fine_bias[64:65], coarse_bias[0:1], up_bias[64:65]], axis=0)


def local(
    features,
    cotangent,
    edge_src,
    send_rows,
    fine_to_coarse,
    coarse_to_fine,
    coarse_edges,
    edge_in,
    edge_out,
    node_in,
    node_out,
    coarse_in,
    coarse_out,
    coarse_mix,
    up_in,
    up_out,
    biases,
):
    scale = (COARSE / (features.shape[1] * lax.axis_size("gx") * lax.axis_size("gy"))) ** 0.5
    factor = (COARSE / coarse_edges.shape[1]) ** 0.5
    f32, dma = jnp.float32, pltpu.SemaphoreType.DMA
    to_coarse, to_fine = fine_to_coarse.reshape(1, -1), coarse_to_fine.reshape(1, -1)
    table = pltpu.VMEM((EXT // RADIX * 64, 2 * RADIX), jnp.bfloat16)
    sums, columns = pltpu.VMEM((EXT // RADIX * 64, RADIX), f32), pltpu.VMEM((8, 2048, 1), f32)
    wide, half = pltpu.VMEM((64, 2048), f32), pltpu.VMEM((32, 2048), f32)
    slots = pltpu.VMEM((4, 64, 128), f32)
    halo = exchange(features, send_rows)
    middle, slope, hidden, node_pre, pooled = remote_call(
        partial(fine_forward_kernel, scale),
        [(64, 2048), (8, 64, 2048), (64, 2048), (64, 2048), (64, 2048)],
        [table, wide, columns, pltpu.VMEM((16, 64, 128), f32), pltpu.VMEM((64, 512), f32), *sum_scratch(16)], 2,
        features, halo, edge_src, to_coarse, edge_in, edge_out, node_in, node_out, biases)
    output, grad_middle, grad_mixed, mixed_back, mixed_sum, up_grads = remote_call(
        partial(coarse_kernel, factor),
        [(64, 2048), (64, 2048), (64, 2048), (64, 2048), (64, 2048), (2, 64, 128)],
        [table, wide, sums, columns, pltpu.VMEM((16, 64, 128), f32), half, half, half, half, dma((4,)),
         *sum_scratch(16)], 3,
        pooled, coarse_in, coarse_out, coarse_mix, biases, coarse_edges, to_fine, middle, cotangent, up_in, up_out)
    grad_features, weight_sums, coarse_grads = remote_call(
        partial(backward_kernel, factor, scale),
        [(64, 2048), (8, 64, 128), (64, 384)],
        [table, wide, wide, sums, columns, wide, slots, pltpu.VMEM((8, 64, 128), f32), slots, dma((4,)), dma((4,)),
         *sum_scratch(8)], 4,
        grad_mixed, mixed_back, mixed_sum, pooled, coarse_in, coarse_out, coarse_mix, biases, to_coarse,
        grad_middle, node_pre, hidden, slope, features, halo, edge_src, edge_in, edge_out, node_in, node_out,
        up_grads, send_rows)
    (out, out_features, grad_edge_in, grad_edge_out, grad_node_in, grad_node_out, grad_coarse_in, grad_coarse_out,
     grad_coarse_mix, grad_up_in, grad_up_out, grad_biases) = call(
        unpack_kernel,
        [(64, 2048), (64, 2048), (64, 128), (64, 64), (64, 128), (64, 64), (64, 64), (64, 64), (64, 64), (64, 128),
         (64, 64), (4, 64)], [], output, grad_features, weight_sums, coarse_grads)
    return (out, out_features, grad_edge_in, grad_edge_out, grad_node_in, grad_node_out, grad_coarse_in,
            grad_coarse_out, grad_coarse_mix, grad_up_in, grad_up_out, grad_biases)


def solution(mesh):
    in_specs = (
        P(None, ("gx", "gy")),
        P(None, ("gx", "gy")),
        P(None, ("gx", "gy")),
        P(None, ("gx", "gy")),
        P(("gx", "gy")),
        P(("gx", "gy")),
        P(),
        P(),
        P(),
        P(),
        P(),
        P(),
        P(),
        P(),
        P(),
        P(),
        P(),
    )
    out_specs = (
        P(None, ("gx", "gy")),
        P(None, ("gx", "gy")),
        P(),
        P(),
        P(),
        P(),
        P(),
        P(),
        P(),
        P(),
        P(),
        P(),
    )
    return jax.shard_map(local, mesh=mesh, in_specs=in_specs, out_specs=out_specs, check_vma=False)
```
